512 devices in a mesh: section: 16 (over z_hi, x, core), seq: 32 (over y, z_lo).
Axes of the slice: x: 4, y: 8, z: 8 (z_hi: 2, z_lo: 4; z = z_hi * 4 + z_lo), core: 2. Of those that a mesh axis runs over, the one named last changes fastest.
Arguments:
- fresh_tokens: bfloat16 [3, 4096, 1024], P(None, 'seq'), may hold values from -6 to 6
- fresh_mask: int32 [3, 4096], P(None, 'seq'), may hold values 0 or 1
- curve_order: int32 [3, 4096], P(None, 'seq'), may hold values from 0 to 4095, as said below
- held_state: bfloat16 [16, 4096, 1024], P('section', 'seq'), may hold values from -6 to 6
- held_mask: int32 [16, 4096], P('section', 'seq'), may hold values 0 or 1
- norm_gains: float32 [16, 1024], P('section'), may hold values from 0.5 to 1.5
- projections: bfloat16 [16, 4, 1024, 512], P('section', None, 'seq'), may hold values from -4 to 4
- mlp_gains: float32 [16, 1024], P('section'), may hold values from 0.5 to 1.5
- mlp_up: bfloat16 [16, 1024, 2048], P('section', 'seq'), may hold values from -0.1875 to 0.1875
- mlp_down: bfloat16 [16, 1024, 2048], P('section', 'seq'), may hold values from -0.125 to 0.125
Outputs:
- section_outputs: bfloat16 [4, 16, 4096, 1024], P(None, 'section', 'seq')
The draws below stay inside these ranges and needn't reach their ends.
Inputs may be any that keep to these rules, and one draw needn't show every extreme that they name: `curve_order`: each aligned block of 128 positions is a permutation of the same block of scene tokens.
All inputs are finite; a program needn't handle non-finite values. No bound on the sum of `fresh_mask` or of `held_mask` on one device may be relied on, other than what follows from the above.
Results may differ from the reference program's by a relative error of at most 0.018.
Values may be sent and summed in bfloat16 or wider, within the bound.
No kernel may reach another device: no remote copies, remote signals or barrier semaphores. Data moves between devices by JAX's collectives and lax.ppermute only.
A program may use at most 64 MiB of HBM per device.

```python
import jax
import jax.numpy as jnp
from jax import lax

D = 1024
HEADS = 8
HEAD = 64
INNER = 512
FF = 2048
HALO = 64
TOK_DEV = 128
TICKS = 4
FEEDS = 3
SECTIONS = 16
TOKENS = 4096


def draw_curve_order(key, part):
    blocks = TOKENS // TOK_DEV
    keys = jax.random.split(key, FEEDS * blocks)
    perms = jax.vmap(lambda subkey: jax.random.permutation(subkey, TOK_DEV))(keys).astype(jnp.int32)
    perms = perms.reshape(FEEDS, blocks, TOK_DEV)
    starts = (jnp.arange(blocks, dtype=jnp.int32) * TOK_DEV)[None, :, None]
    return (perms + starts).reshape(FEEDS, TOKENS).astype(jnp.int32)


def draw_projections(key, part):
    key_base = jax.random.fold_in(key, 11)
    key_other = jax.random.fold_in(key, 23)
    base = jax.random.truncated_normal(key_base, -4.0, 4.0, (SECTIONS, 3, D, INNER), jnp.float32) * D ** (-0.5)
    other = jax.random.truncated_normal(key_other, -4.0, 4.0, (SECTIONS, 1, D, INNER), jnp.float32) * (3.0 * INNER ** (-0.5))
    return jnp.concatenate([base, other], axis=1).astype(jnp.bfloat16)


def plant(entries, rng, least, top_value):
    spot = [jax.random.randint(jax.random.fold_in(rng, axis), (), 0, length) for axis, length in enumerate(entries.shape)]
    longest = entries.shape.index(max(entries.shape))
    neighbour = spot[:longest] + [(spot[longest] + 1) % entries.shape[longest]] + spot[longest + 1:]
    return entries.at[tuple(spot)].set(least).at[tuple(neighbour)].set(top_value)


def block_scale(rng, shape, cuts, smallest, top_value):
    level, own = 1.0, jax.random.fold_in(rng, 6)
    for position, blocks in cuts:
        steps = jnp.exp(jax.random.uniform(jax.random.fold_in(own, position), (blocks,), jnp.float32, smallest / len(cuts), top_value / len(cuts)))
        level = level * jnp.repeat(steps, shape[position] // blocks).reshape([-1 if axis == position else 1 for axis in range(len(shape))])
    return level


def gaussian(rng, extent, spread, most, shards=(), kind=jnp.bfloat16):
    result = jax.random.normal(rng, extent, jnp.float32) * spread
    if len(shards) > 0:
        result = block_scale(rng, extent, shards, -0.22, 0.18) * result
    return jnp.clip(result, min=-most, max=most).astype(kind)


def setup_inputs(seed: int = 0) -> dict:
    arg_keys = jax.random.split(jax.random.key(seed), 11)
    return {
        "fresh_tokens": gaussian(arg_keys[0], (FEEDS, TOKENS, D), 1.0, 6.0, ((1, 32),)),
        "fresh_mask": plant((jax.random.randint(arg_keys[1], (FEEDS, TOKENS), 0, 5) < 2).astype(jnp.int32), jax.random.fold_in(arg_keys[1], 1), 0, 1),
        "curve_order": draw_curve_order(jax.random.fold_in(arg_keys[10], 71), 0),
        "held_state": gaussian(arg_keys[3], (SECTIONS, TOKENS, D), 1.0, 6.0, ((0, 16), (1, 32))),
        "held_mask": plant((jax.random.randint(arg_keys[4], (SECTIONS, TOKENS), 0, 5) < 2).astype(jnp.int32), jax.random.fold_in(arg_keys[4], 1), 0, 1),
        "norm_gains": jnp.clip(0.5 + 1.0 * jax.random.uniform(arg_keys[5], (SECTIONS, D), jnp.float32) ** block_scale(arg_keys[5], (SECTIONS, D), ((0, 16),), -0.2, 0.2), 0.5, 1.5),
        "projections": draw_projections(jax.random.fold_in(arg_keys[10], 71), 0),
        "mlp_gains": jnp.clip(0.5 + 1.0 * jax.random.uniform(arg_keys[7], (SECTIONS, D), jnp.float32) ** block_scale(arg_keys[7], (SECTIONS, D), ((0, 16),), -0.2, 0.2), 0.5, 1.5),
        "mlp_up": gaussian(arg_keys[8], (SECTIONS, D, FF), D ** -0.5, 0.1875, ((0, 16), (1, 32))),
        "mlp_down": gaussian(arg_keys[9], (SECTIONS, D, FF), FF ** -0.5, 0.125, ((0, 16), (1, 32))),
    }


def normalize(current, gain):
    values = current.astype(jnp.float32)
    average = lax.optimization_barrier(jnp.mean(values, axis=-1, keepdims=True))
    centered = values - average
    spread_sq = lax.optimization_barrier(jnp.mean(centered * centered, axis=-1, keepdims=True))
    return (centered * lax.rsqrt(spread_sq + 1e-05) * gain).astype(jnp.bfloat16)

def attend(queries, keys_vals, visible_ext):
    count = queries.shape[0]
    length = keys_vals.shape[0]
    reach = (length - count) // 2
    q_heads = queries.astype(jnp.float32).reshape(count, HEADS, HEAD)
    k_heads = keys_vals[:, :INNER].astype(jnp.float32).reshape(length, HEADS, HEAD)
    v_heads = keys_vals[:, INNER:].astype(jnp.float32).reshape(length, HEADS, HEAD)
    scores = jnp.einsum('rhd,lhd->hrl', q_heads, k_heads) * HEAD ** (-0.5)
    row_pos = jnp.arange(count, dtype=jnp.int32)[:, None]
    col_pos = jnp.arange(length, dtype=jnp.int32)[None, :] - reach
    allowed = (jnp.abs(col_pos - row_pos) <= reach) & ((visible_ext[None, :] == 1) | (col_pos == row_pos))
    scores = jnp.where(allowed[None], scores, jnp.float32(-1e+30))
    highest = lax.optimization_barrier(jnp.max(scores, axis=-1, keepdims=True))
    exps = jnp.exp(scores - highest)
    totals = lax.optimization_barrier(jnp.sum(exps, axis=-1, keepdims=True))
    shares = (exps / totals).astype(jnp.bfloat16)
    context = jnp.einsum('hrl,lhd->rhd', shares.astype(jnp.float32), v_heads)
    return context.reshape(count, INNER).astype(jnp.bfloat16)

def feed_forward(attended, gain, w_up, w_down):
    normed = normalize(attended, gain)
    hidden = jnp.dot(normed, w_up, preferred_element_type=jnp.float32)
    hidden = jax.nn.gelu(hidden, approximate=False).astype(jnp.bfloat16)
    projected = lax.dot_general(hidden, w_down, (((1,), (1,)), ((), ())), preferred_element_type=jnp.float32)
    return (attended.astype(jnp.float32) + projected).astype(jnp.bfloat16)

def encoder_block(current, visible, gain, weights, gain_mlp, w_up, w_down):
    normed = normalize(current, gain)
    queries = jnp.dot(normed, weights[0], preferred_element_type=jnp.float32).astype(jnp.bfloat16)
    keys = jnp.dot(normed, weights[1], preferred_element_type=jnp.float32).astype(jnp.bfloat16)
    values = jnp.dot(normed, weights[2], preferred_element_type=jnp.float32).astype(jnp.bfloat16)
    joined = jnp.concatenate([keys, values], axis=1)
    padded = jnp.pad(joined, ((HALO, HALO), (0, 0)))
    padded_mask = jnp.pad(visible, (HALO, HALO))

    def one_block(block_idx):
        offset = (block_idx * TOK_DEV).astype(jnp.int32)
        q_block = lax.dynamic_slice_in_dim(queries, offset, TOK_DEV, 0)
        kv_block = lax.dynamic_slice_in_dim(padded, offset, TOK_DEV + 2 * HALO, 0)
        m_block = lax.dynamic_slice_in_dim(padded_mask, offset, TOK_DEV + 2 * HALO, 0)
        return attend(q_block, kv_block, m_block)
    context = lax.map(one_block, jnp.arange(TOKENS // TOK_DEV, dtype=jnp.int32))
    context = context.reshape(TOKENS, INNER)
    projected = lax.dot_general(context, weights[3], (((1,), (1,)), ((), ())), preferred_element_type=jnp.float32)
    attended = (current.astype(jnp.float32) + projected).astype(jnp.bfloat16)
    return feed_forward(attended, gain_mlp, w_up, w_down)

def run_section(operands):
    return encoder_block(*operands)

def reference(fresh_tokens, fresh_mask, curve_order, held_state, held_mask, norm_gains, projections, mlp_gains, mlp_up, mlp_down):
    serial_tokens = jax.vmap(lambda source, indices: jnp.take(source, indices, axis=0))(fresh_tokens, curve_order)
    serial_mask = jax.vmap(lambda source, indices: jnp.take(source, indices, axis=0))(fresh_mask, curve_order)
    states = held_state
    masks = held_mask
    gathered = []
    for tick in range(TICKS):
        results = lax.map(run_section, (states, masks, norm_gains, projections, mlp_gains, mlp_up, mlp_down))
        gathered.append(results)
        if tick < TICKS - 1:
            states = jnp.concatenate([serial_tokens[tick][None], results[:-1]], axis=0)
            masks = jnp.concatenate([serial_mask[tick][None], masks[:-1]], axis=0)
    return jnp.stack(gathered)
```

```python
import functools

import jax
import jax.numpy as jnp
from jax import lax
from jax.experimental import pallas as pl
from jax.experimental.pallas import tpu as pltpu
from jax.sharding import Mesh, PartitionSpec as P

HEADS = 8
HEAD = 64
INNER = 512
HALO = 64
TICKS = 4
ZL = 4
TILE = 512
SEQ = ("y", "z")


def _normed(values, gain):
    average = jnp.mean(values, axis=-1, keepdims=True)
    centered = values - average
    spread_sq = jnp.mean(centered * centered, axis=-1, keepdims=True)
    return (centered * lax.rsqrt(spread_sq + 1e-05) * gain).astype(jnp.bfloat16)


def _dot(a, b, dims):
    return lax.dot_general(a, b, (dims, ((), ())), preferred_element_type=jnp.float32)


def tick_kernel(t, flags_ref, ext_ref, seen_ref, gain_ref, gain_mlp_ref,
                w_own_ref, w_pair_ref, w_two_ref, *refs):
    relayed = refs[:-9]
    out_ref, first_ref, last_ref, weights, qkv, context, normed, hidden, sems = refs[-9:]
    count = out_ref.shape[0]
    length = ext_ref.shape[1]
    my_z = flags_ref[1]

    def copies(a):
        spots = (my_z, my_z + 1 - 2 * lax.rem(my_z, 2), lax.rem(my_z + 2, ZL), ZL - 1 - my_z)
        pieces = (w_own_ref.at[:, a], w_pair_ref.at[:, a], w_two_ref.at[:, 0, a], w_two_ref.at[:, 1, a])
        found = [
            pltpu.make_async_copy(piece, weights.at[a, :, spot], sems.at[a, k])
            for k, (piece, spot) in enumerate(zip(pieces, spots))
        ]
        return found

    for a in range(3):
        for copy in copies(a):
            copy.start()

    def fetch():
        copy = pltpu.make_async_copy(ext_ref.at[t], context, sems.at[3, 0])
        copy.start()
        copy.wait()

    if relayed:
        before_ref, passed_ref, after_ref = relayed
        is_first = flags_ref[0] == 1
        pl.when(is_first)(fetch)

        @pl.when(jnp.logical_not(is_first))
        def _():
            context[:HALO] = before_ref[...]
            context[HALO:HALO + count] = passed_ref[...]
            context[HALO + count:] = after_ref[...]
    else:
        fetch()
    normed[...] = _normed(context[...].astype(jnp.float32), gain_ref[...])
    for copy in copies(0):
        copy.wait()

    def rows_of(a, lo, hi):
        w = weights[a, :, :, :, lo:hi]
        return w.reshape(-1, hi - lo)

    for n in range(3):
        qkv[:, n * INNER:(n + 1) * INNER] = _dot(
            normed[...], rows_of(0, n * INNER, (n + 1) * INNER), ((1,), (0,))).astype(jnp.bfloat16)

    row = lax.broadcasted_iota(jnp.int32, (count, length), 0)
    col = lax.broadcasted_iota(jnp.int32, (count, length), 1) - HALO
    allowed = (jnp.abs(col - row) <= HALO) & ((seen_ref[t:t + 1, :] == 1) | (col == row))
    bias = jnp.where(allowed, 0.0, -1e30)
    bias = jnp.concatenate([bias, bias], axis=0)
    lane = lax.broadcasted_iota(jnp.int32, (count, 2 * HEAD), 1)
    parts = []
    for pair in range(HEADS // 2):
        lo = pair * 2 * HEAD
        q = qkv[HALO:HALO + count, lo:lo + 2 * HEAD]
        k = qkv[:, INNER + lo:INNER + lo + 2 * HEAD]
        v = qkv[:, 2 * INNER + lo:2 * INNER + lo + 2 * HEAD]
        zero = jnp.zeros_like(q)
        both = jnp.concatenate([jnp.where(lane < HEAD, q, zero), jnp.where(lane < HEAD, zero, q)], axis=0)
        scores = _dot(both, k, ((1,), (1,))) * HEAD ** (-0.5)
        scores = jnp.where(bias < 0, jnp.float32(-1e30), scores)
        highest = jnp.max(scores, axis=-1, keepdims=True)
        exps = jnp.exp(scores - highest)
        totals = jnp.sum(exps, axis=-1, keepdims=True)
        shares = (exps / totals).astype(jnp.bfloat16)
        mixed = _dot(shares, v, ((1,), (0,)))
        parts.append(jnp.where(lane < HEAD, mixed[:count], mixed[count:]).astype(jnp.bfloat16))
    mixed = jnp.concatenate(parts, axis=1)
    attended = context[HALO:HALO + count].astype(jnp.float32) + _dot(
        mixed, rows_of(0, 3 * INNER, 4 * INNER), ((1,), (1,)))
    attended = attended.astype(jnp.bfloat16)
    context[:count] = attended
    normed[:count] = _normed(attended.astype(jnp.float32), gain_mlp_ref[...])
    for copy in copies(1):
        copy.wait()
    for n in range(hidden.shape[1] // TILE):
        lo = n * TILE
        up = _dot(normed[:count], rows_of(1, lo, lo + TILE), ((1,), (0,)))
        up = 0.5 * up * (1.0 + lax.erf(up * (0.5 ** 0.5)))
        hidden[:, lo:lo + TILE] = up.astype(jnp.bfloat16)
    for copy in copies(2):
        copy.wait()
    groups = weights.shape[1]
    for g in range(0, groups, 2):
        w = weights[2, g:g + 2]
        w = w.reshape(-1, w.shape[-1])
        wide = w.shape[0]
        lo = g * wide // 2
        result = (context[:count, lo:lo + wide].astype(jnp.float32) + _dot(
            hidden[...], w, ((1,), (1,)))).astype(jnp.bfloat16)
        out_ref[:, lo:lo + wide] = result
        first_ref[:, lo:lo + wide] = result[:HALO]
        last_ref[:, lo:lo + wide] = result[count - HALO:]


def tick(t, flags, ext, seen, gain, gain_mlp, w_own, w_pair, w_two, relayed):
    _, length, width = ext.shape
    count = length - 2 * HALO
    rows, _, depth, wide = w_own.shape
    vmem = pl.BlockSpec(memory_space=pltpu.VMEM)
    anyw = pl.BlockSpec(memory_space=pl.ANY)
    return pl.pallas_call(
        functools.partial(tick_kernel, t),
        out_shape=(jax.ShapeDtypeStruct((count, width), jnp.bfloat16),
                   jax.ShapeDtypeStruct((HALO, width), jnp.bfloat16),
                   jax.ShapeDtypeStruct((HALO, width), jnp.bfloat16)),
        in_specs=[pl.BlockSpec(memory_space=pltpu.SMEM), anyw] + [vmem] * 3
        + [anyw] * 3 + [vmem] * len(relayed),
        out_specs=(vmem, vmem, vmem),
        scratch_shapes=[
            pltpu.VMEM((3, rows, ZL, depth, wide), jnp.bfloat16),
            pltpu.VMEM((length, 3 * INNER), jnp.bfloat16),
            pltpu.VMEM((length, width), jnp.bfloat16),
            pltpu.VMEM((length, width), jnp.bfloat16),
            pltpu.VMEM((count, wide), jnp.bfloat16),
            pltpu.SemaphoreType.DMA((4, ZL)),
        ],
        compiler_params=pltpu.CompilerParams(vmem_limit_bytes=24 * 1024 * 1024),
        name="tick",
    )(flags, ext, seen, gain, gain_mlp, w_own, w_pair, w_two, *relayed)


def gather_rows(own):
    rows = lax.axis_size("y")

    def swapped(value, mask):
        return lax.ppermute(value, "z", [(z, z ^ mask) for z in range(ZL)])

    w_own = lax.all_gather(own, "y")
    two = jnp.stack([swapped(own, 2), swapped(own, 3)])
    w_two = lax.all_gather(two, "y")
    w_pair = swapped(w_own, 1)
    return w_own, w_pair, w_two


def body(
    fresh_tokens,
    fresh_mask,
    curve_order,
    held_state,
    held_mask,
    norm_gains,
    projections,
    mlp_gains,
    mlp_up,
    mlp_down,
):
    sections, seqs = lax.axis_size("section"), lax.axis_size(SEQ)
    section = lax.axis_index("section")
    is_first = section == 0
    count = held_state.shape[1]

    own = jnp.stack([
        projections[0].transpose(1, 0, 2).reshape(projections.shape[2], 4 * INNER),
        mlp_up[0],
        mlp_down[0],
    ])
    w_own, w_pair, w_two = gather_rows(own)

    up = [(i, i + 1) for i in range(seqs - 1)]
    down = [(i + 1, i) for i in range(seqs - 1)]

    def padded(value, axis, names, up, down):
        size = value.shape[axis]
        before = lax.ppermute(lax.slice_in_dim(value, size - HALO, size, axis=axis), names, up)
        after = lax.ppermute(lax.slice_in_dim(value, 0, HALO, axis=axis), names, down)
        return jnp.concatenate([before, value, after], axis=axis)

    local_order = curve_order - lax.axis_index(SEQ) * count
    serial_tokens = jax.vmap(lambda source, indices: jnp.take(source, indices, axis=0))(
        fresh_tokens, local_order
    )
    serial_mask = jnp.take_along_axis(fresh_mask, local_order, axis=1)

    ext = jnp.concatenate([
        padded(held_state, 1, SEQ, up, down),
        padded(serial_tokens, 1, ("section",) + SEQ, up, down),
    ])
    masks_ext = padded(jnp.concatenate([held_mask, serial_mask]), 1, SEQ, up, down)
    visible = [masks_ext[0]]
    onward = [(i, i + 1) for i in range(sections - 1)]
    for t in range(1, TICKS):
        passed = lax.ppermute(visible[-1], "section", onward)
        visible.append(jnp.where(is_first, masks_ext[t], passed))
    seen = jnp.stack(visible)

    def relay(shift):
        return [
            (s * seqs + j, (s + 1) * seqs + j + shift)
            for s in range(sections - 1) for j in range(seqs) if 0 <= j + shift < seqs
        ]

    every = ("section",) + SEQ
    flags = jnp.stack([is_first.astype(jnp.int32), lax.axis_index("z").astype(jnp.int32)])
    results = []
    relayed = ()
    for t in range(TICKS):
        result, first, last = tick(
            t, flags, ext, seen, norm_gains, mlp_gains, w_own, w_pair, w_two, relayed)
        results.append(result)
        if t < TICKS - 1:
            relayed = (
                lax.ppermute(last, every, relay(1)),
                lax.ppermute(result, every, relay(0)),
                lax.ppermute(first, every, relay(-1)),
            )
    return jnp.stack(results)[:, None]


def solution(mesh):
    sections, seqs = mesh.shape["section"], mesh.shape["seq"]
    split = Mesh(mesh.devices.reshape(sections, seqs // ZL, ZL), ("section",) + SEQ)
    return jax.shard_map(
        body,
        mesh=split,
        in_specs=(
            P(None, SEQ, None),
            P(None, SEQ),
            P(None, SEQ),
            P("section", SEQ, None),
            P("section", SEQ),
            P("section", None),
            P("section", None, SEQ, None),
            P("section", None),
            P("section", SEQ, None),
            P("section", SEQ, None),
        ),
        out_specs=P(None, "section", SEQ, None),
        check_vma=False,
    )
```

```python
import functools

import jax
import jax.numpy as jnp
from jax import lax
from jax.experimental import pallas as pl
from jax.experimental.pallas import tpu as pltpu
from jax.sharding import Mesh, PartitionSpec as P

HEADS = 8
HEAD = 64
INNER = 512
HALO = 64
TICKS = 4
ZL = 4
TILE = 512
MARKS = 16
SEQ = ("y", "z")


def _normed(values, gain):
    average = jnp.mean(values, axis=-1, keepdims=True)
    centered = values - average
    spread_sq = jnp.mean(centered * centered, axis=-1, keepdims=True)
    return (centered * lax.rsqrt(spread_sq + 1e-05) * gain).astype(jnp.bfloat16)


def _dot(a, b, dims):
    return lax.dot_general(a, b, (dims, ((), ())), preferred_element_type=jnp.float32)


def tick_kernel(t, spots, flags_ref, gain_ref, gain_mlp_ref, *refs):
    before_ref, main_ref, after_ref = refs[:3]
    refs = refs[3:]
    feeds = ()
    if t > 0:
        feeds, refs = refs[:3], refs[3:]
        weights, refs = refs[0], refs[1:]
        copies = None
    else:
        pieces, refs = refs[:len(spots)], refs[len(spots):]
    out_ref, before_out, main_out, after_out = refs[:4]
    refs = refs[4:]
    if t == 0:
        weights, refs = refs[0], refs[1:]
        my_y, my_z = flags_ref[1], flags_ref[2]
        rows = weights.shape[1]

        def copies(a):
            found, slot = [], 0
            for piece, places in zip(pieces, spots):
                for i, (delta, mask) in enumerate(places):
                    y = lax.rem(my_y + (delta + rows), rows)
                    z = (my_z, my_z + 1 - 2 * lax.rem(my_z, 2), lax.rem(my_z + 2, ZL), ZL - 1 - my_z)[mask]
                    source = piece.at[a] if len(places) == 1 else piece.at[i, a]
                    found.append(pltpu.make_async_copy(source, weights.at[a, y, z], sems.at[a, slot]))
                    slot += 1
            return found

    qkv, context, marks, normed, hidden, sems = refs
    count = out_ref.shape[0]
    length = count + 2 * HALO

    if t == 0:
        for a in range(3):
            for copy in copies(a):
                copy.start()

    places = ((0, HALO), (HALO, count), (HALO + count, HALO))

    def relayed():
        for i, (ref, (at, size)) in enumerate(zip((before_ref, main_ref, after_ref), places)):
            context[at:at + size] = ref[:size]
            marks[i] = ref[size:]

    if feeds:
        is_first = flags_ref[0] == 1

        @pl.when(is_first)
        def _():
            fetched = []
            for i, (ref, (at, size)) in enumerate(zip(feeds, places)):
                fetched.append(pltpu.make_async_copy(
                    ref.at[t - 1, :size], context.at[at:at + size], sems.at[0, 2 * i]))
                fetched.append(pltpu.make_async_copy(
                    ref.at[t - 1, size:], marks.at[i], sems.at[0, 2 * i + 1]))
            for copy in fetched:
                copy.start()
            for copy in fetched:
                copy.wait()

        pl.when(jnp.logical_not(is_first))(relayed)
    else:
        relayed()

    wide = 2 * HALO + count
    seen = sum(marks[i, 0:1, :wide].astype(jnp.float32) for i in range(3))
    normed[...] = _normed(context[...].astype(jnp.float32), gain_ref[...])

    def wait(a):
        if t == 0:
            for copy in copies(a):
                copy.wait()

    def columns(a, lo, hi):
        return weights[a, :, :, :, lo:hi].reshape(-1, hi - lo)

    wait(0)
    for n in range(3):
        qkv[:, n * INNER:(n + 1) * INNER] = _dot(
            normed[...], columns(0, n * INNER, (n + 1) * INNER), ((1,), (0,))).astype(jnp.bfloat16)

    row = lax.broadcasted_iota(jnp.int32, (count, length), 0)
    col = lax.broadcasted_iota(jnp.int32, (count, length), 1) - HALO
    allowed = (jnp.abs(col - row) <= HALO) & ((seen > 0.5) | (col == row))
    barred = jnp.where(allowed, 0.0, 1.0)
    barred = jnp.concatenate([barred, barred], axis=0) > 0.5
    lane = lax.broadcasted_iota(jnp.int32, (count, 2 * HEAD), 1)
    parts = []
    for pair in range(HEADS // 2):
        lo = pair * 2 * HEAD
        q = qkv[HALO:HALO + count, lo:lo + 2 * HEAD]
        k = qkv[:, INNER + lo:INNER + lo + 2 * HEAD]
        v = qkv[:, 2 * INNER + lo:2 * INNER + lo + 2 * HEAD]
        zero = jnp.zeros_like(q)
        both = jnp.concatenate(
            [jnp.where(lane < HEAD, q, zero), jnp.where(lane < HEAD, zero, q)], axis=0)
        scores = _dot(both, k, ((1,), (1,))) * HEAD ** (-0.5)
        scores = jnp.where(barred, jnp.float32(-1e30), scores)
        highest = jnp.max(scores, axis=-1, keepdims=True)
        exps = jnp.exp(scores - highest)
        totals = jnp.sum(exps, axis=-1, keepdims=True)
        shares = (exps / totals).astype(jnp.bfloat16)
        mixed = _dot(shares, v, ((1,), (0,)))
        parts.append(jnp.where(lane < HEAD, mixed[:count], mixed[count:]).astype(jnp.bfloat16))
    attended = context[HALO:HALO + count].astype(jnp.float32) + _dot(
        jnp.concatenate(parts, axis=1), columns(0, 3 * INNER, 4 * INNER), ((1,), (1,)))
    attended = attended.astype(jnp.bfloat16)
    context[:count] = attended
    normed[:count] = _normed(attended.astype(jnp.float32), gain_mlp_ref[...])
    wait(1)
    for lo in range(0, hidden.shape[1], TILE):
        up = _dot(normed[:count], columns(1, lo, lo + TILE), ((1,), (0,)))
        up = 0.5 * up * (1.0 + lax.erf(up * (0.5 ** 0.5)))
        hidden[:, lo:lo + TILE] = up.astype(jnp.bfloat16)
    wait(2)
    for g in range(0, weights.shape[1], 2):
        w = weights[2, g:g + 2]
        w = w.reshape(-1, w.shape[-1])
        size = w.shape[0]
        lo = g * size // 2
        result = (context[:count, lo:lo + size].astype(jnp.float32) + _dot(
            hidden[...], w, ((1,), (1,)))).astype(jnp.bfloat16)
        out_ref[:, lo:lo + size] = result
        if t < TICKS - 1:
            main_out[:count, lo:lo + size] = result
            after_out[:HALO, lo:lo + size] = result[:HALO]
            before_out[:HALO, lo:lo + size] = result[count - HALO:]
    if t < TICKS - 1:
        at = lax.broadcasted_iota(jnp.int32, (MARKS, count), 1)
        left = jnp.broadcast_to(seen[:, :count], (MARKS, count))
        right = jnp.broadcast_to(seen[:, count:], (MARKS, count))
        none = jnp.zeros((MARKS, count), jnp.float32)
        left = jnp.where(at >= HALO, left, none)
        right = jnp.where(at < HALO, right, none)
        for ref, lows, highs in (
            (before_out, right, none), (main_out, left, right), (after_out, none, left)
        ):
            size = ref.shape[0] - MARKS
            ref[size:] = jnp.zeros((MARKS, ref.shape[1]), ref.dtype)
            ref[size:, :count] = lows.astype(ref.dtype)
            ref[size:, count:2 * count] = highs.astype(ref.dtype)


def tick(t, flags, gain, gain_mlp, payload, feeds, weights, spots, shape):
    width = payload[0].shape[1]
    count = payload[1].shape[0] - MARKS
    length = count + 2 * HALO
    hidden = shape[-1]
    vmem = pl.BlockSpec(memory_space=pltpu.VMEM)
    anyw = pl.BlockSpec(memory_space=pl.ANY)
    small = ((HALO, count, HALO) if t < TICKS - 1 else (0, 0, 0))
    outs = [jax.ShapeDtypeStruct((count, width), jnp.bfloat16)]
    outs += [jax.ShapeDtypeStruct((size + MARKS, width), jnp.bfloat16) for size in small]
    if t == 0:
        outs.append(jax.ShapeDtypeStruct(shape, jnp.bfloat16))
        operands, specs = list(payload) + list(weights), [vmem] * 3 + [anyw] * len(weights)
    else:
        operands = list(payload) + list(feeds) + [weights]
        specs = [vmem] * 3 + [anyw] * 3 + [vmem]
    slots = max(8, sum(len(p) for p in spots))
    return pl.pallas_call(
        functools.partial(tick_kernel, t, spots),
        out_shape=tuple(outs),
        in_specs=[pl.BlockSpec(memory_space=pltpu.SMEM), vmem, vmem] + specs,
        out_specs=tuple([vmem] * len(outs)),
        scratch_shapes=[
            pltpu.VMEM((length, 3 * INNER), jnp.bfloat16),
            pltpu.VMEM((length, width), jnp.bfloat16),
            pltpu.VMEM((3, MARKS, width), jnp.bfloat16),
            pltpu.VMEM((length, width), jnp.bfloat16),
            pltpu.VMEM((count, hidden), jnp.bfloat16),
            pltpu.SemaphoreType.DMA((3, slots)),
        ],
        compiler_params=pltpu.CompilerParams(vmem_limit_bytes=22 * 1024 * 1024),
        name=f"tick{t}",
    )(flags, gain, gain_mlp, *operands)


def gather_rows(own):
    rows = lax.axis_size("y")
    far = rows // 2

    def swapped(value, mask):
        return lax.ppermute(value, "z", [(z, z ^ mask) for z in range(ZL)])

    def moved(value, delta):
        return lax.ppermute(value, "y", [(y, (y + delta) % rows) for y in range(rows)])

    held = {0: {0: own}, 2: {0: swapped(own, 2)}, 3: {0: swapped(own, 3)}}
    for step in range(1, far):
        for chunks in held.values():
            chunks[-step] = moved(chunks[1 - step], 1)
            chunks[step] = moved(chunks[step - 1], -1)
    for mask, chunks in held.items():
        chunks[far] = moved(chunks[far - 1], -1) if mask == 2 else moved(chunks[1 - far], 1)
    pieces, spots = [], []
    for mask, chunks in held.items():
        for delta, piece in chunks.items():
            pieces.append(piece)
            spots.append(((delta, mask),))
    for group in ((0, -1, 1), (-2, 2), (-3, 3, far)):
        pieces.append(swapped(jnp.stack([held[0][delta] for delta in group]), 1))
        spots.append(tuple((delta, 1) for delta in group))
    return pieces, spots, held


def body(
    fresh_tokens,
    fresh_mask,
    curve_order,
    held_state,
    held_mask,
    norm_gains,
    projections,
    mlp_gains,
    mlp_up,
    mlp_down,
):
    sections, seqs = lax.axis_size("section"), lax.axis_size(SEQ)
    is_first = lax.axis_index("section") == 0
    count, width = held_state.shape[1:]
    depth = projections.shape[2]

    own = jnp.stack([
        projections[0].transpose(1, 0, 2).reshape(depth, 4 * INNER),
        mlp_up[0],
        mlp_down[0],
    ])
    pieces, spots, held = gather_rows(own)
    shape = (3, seqs // ZL, ZL, depth, own.shape[2])

    def payloads(tokens, mask, names):
        mask = mask.astype(jnp.bfloat16)

        def marked(part, seen, at):
            line = jnp.pad(seen, ((0, 0), (at, width - at - seen.shape[1])))[:, None]
            line = jnp.broadcast_to(line, (part.shape[0], MARKS, width))
            return jnp.concatenate([part, line], axis=1)

        up = [(i, i + 1) for i in range(seqs - 1)]
        down = [(i + 1, i) for i in range(seqs - 1)]
        main = marked(tokens, mask, HALO)
        before = lax.ppermute(marked(tokens[:, count - HALO:], mask[:, count - HALO:], 0), names, up)
        after = lax.ppermute(marked(tokens[:, :HALO], mask[:, :HALO], HALO + count), names, down)
        return before, main, after

    _, held_state, held_mask = lax.optimization_barrier((held[2][-1], held_state, held_mask))
    payload = [part[0] for part in payloads(held_state, held_mask, SEQ)]

    _, fresh_tokens, fresh_mask, curve_order = lax.optimization_barrier(
        (held[0][-2], fresh_tokens, fresh_mask, curve_order))
    local_order = curve_order - lax.axis_index(SEQ) * count
    serial_tokens = jax.vmap(lambda source, indices: jnp.take(source, indices, axis=0))(
        fresh_tokens, local_order
    )
    serial_mask = jnp.take_along_axis(fresh_mask, local_order, axis=1)
    feeds = payloads(serial_tokens, serial_mask, ("section",) + SEQ)

    def relay(shift):
        return [
            (s * seqs + j, (s + 1) * seqs + j + shift)
            for s in range(sections - 1) for j in range(seqs) if 0 <= j + shift < seqs
        ]

    every = ("section",) + SEQ
    flags = jnp.stack([
        is_first.astype(jnp.int32),
        lax.axis_index("y").astype(jnp.int32),
        lax.axis_index("z").astype(jnp.int32),
    ])
    results = []
    weights = pieces
    for t in range(TICKS):
        outs = tick(t, flags, norm_gains, mlp_gains, payload, feeds, weights, spots, shape)
        results.append(outs[0])
        if t == 0:
            weights = outs[4]
        if t < TICKS - 1:
            before, main, after = outs[1:4]
            payload = (
                lax.ppermute(before, every, relay(1)),
                lax.ppermute(main, every, relay(0)),
                lax.ppermute(after, every, relay(-1)),
            )
    return jnp.stack(results)[:, None]


def solution(mesh):
    sections, seqs = mesh.shape["section"], mesh.shape["seq"]
    split = Mesh(mesh.devices.reshape(sections, seqs // ZL, ZL), ("section",) + SEQ)
    return jax.shard_map(
        body,
        mesh=split,
        in_specs=(
            P(None, SEQ, None),
            P(None, SEQ),
            P(None, SEQ),
            P("section", SEQ, None),
            P("section", SEQ),
            P("section", None),
            P("section", None, SEQ, None),
            P("section", None),
            P("section", SEQ, None),
            P("section", SEQ, None),
        ),
        out_specs=P(None, "section", SEQ, None),
        check_vma=False,
    )
```

```python
import functools

import jax
import jax.numpy as jnp
from jax import lax
from jax.experimental import pallas as pl
from jax.experimental.pallas import tpu as pltpu
from jax.sharding import Mesh, PartitionSpec as P

HEADS = 8
HEAD = 64
INNER = 512
HALO = 64
TICKS = 4
ZL = 4
TILE = 512
MARKS = 16
SEQ = ("y", "z")


def _normed(values, gain):
    average = jnp.mean(values, axis=-1, keepdims=True)
    centered = values - average
    spread_sq = jnp.mean(centered * centered, axis=-1, keepdims=True)
    return (centered * lax.rsqrt(spread_sq + 1e-05) * gain).astype(jnp.bfloat16)


def _dot(a, b, dims):
    return lax.dot_general(a, b, (dims, ((), ())), preferred_element_type=jnp.float32)


def chunk_copies(flags_ref, weights, pieces, spots, sems, arrays):
    my_y, my_z = flags_ref[1], flags_ref[2]
    rows = weights.shape[1]
    flipped = my_z + 1 - 2 * lax.rem(my_z, 2)
    columns_at = (my_z, flipped, lax.rem(my_z + 2, ZL), ZL - 1 - my_z)
    found, slot = [], 0
    for piece, places in zip(pieces, spots):
        for i, (delta, mask) in enumerate(places):
            y = lax.rem(my_y + (delta + rows), rows)
            chunk = piece if len(piece.shape) == 3 else piece.at[i]
            found.append(pltpu.make_async_copy(
                chunk.at[arrays], weights.at[arrays, y, columns_at[mask]], sems.at[slot]))
            slot += 1
    return found


def place_kernel(spots, fresh, flags_ref, *refs):
    weights, sems = refs[-2:]
    pieces = refs[:-2] if fresh else refs[1:-2]
    copies = chunk_copies(flags_ref, weights, pieces, spots, sems, slice(None))
    for copy in copies:
        copy.start()
    for copy in copies:
        copy.wait()


def place(flags, weights, pieces, spots, shape, name):
    fresh = weights is None
    vmem = pl.BlockSpec(memory_space=pltpu.VMEM)
    anyw = pl.BlockSpec(memory_space=pl.ANY)
    held = [] if fresh else [weights]
    chunks = sum(len(p) for p in spots)
    moved_bytes = 2 * chunks * shape[0] * shape[3] * shape[4] * 2
    return pl.pallas_call(
        functools.partial(place_kernel, spots, fresh),
        out_shape=jax.ShapeDtypeStruct(shape, jnp.bfloat16),
        in_specs=[pl.BlockSpec(memory_space=pltpu.SMEM)] + [vmem] * len(held) + [anyw] * len(pieces),
        out_specs=vmem,
        input_output_aliases={} if fresh else {1: 0},
        scratch_shapes=[pltpu.SemaphoreType.DMA((chunks,))],
        compiler_params=pltpu.CompilerParams(vmem_limit_bytes=16 * 1024 * 1024),
        cost_estimate=pl.CostEstimate(flops=0, bytes_accessed=moved_bytes, transcendentals=0),
        name=name,
    )(flags, *held, *pieces)


def tick_kernel(t, spots, flags_ref, gain_ref, gain_mlp_ref, *refs):
    before_ref, main_ref, after_ref = refs[:3]
    refs = refs[3:]
    feeds, pieces = (), ()
    if t > 0:
        feeds, refs = refs[:3], refs[3:]
    else:
        pieces, refs = refs[:len(spots)], refs[len(spots):]
    weights, refs = refs[0], refs[1:]
    out_ref, before_out, main_out, after_out = refs[:4]
    refs = refs[4:]
    if t == 0:
        weights, refs = refs[0], refs[1:]
    qkv, context, marks, normed, hidden, sems, place_sems = refs
    count = out_ref.shape[0]
    length = count + 2 * HALO

    def late(a):
        return chunk_copies(flags_ref, weights, pieces, spots, place_sems.at[a], a)

    for a in range(3):
        for copy in late(a):
            copy.start()

    def wait(a):
        for copy in late(a):
            copy.wait()

    places = ((0, HALO), (HALO, count), (HALO + count, HALO))

    def relayed():
        for i, (ref, (at, size)) in enumerate(zip((before_ref, main_ref, after_ref), places)):
            context[at:at + size] = ref[:size]
            marks[i] = ref[size:]

    if feeds:
        is_first = flags_ref[0] == 1

        @pl.when(is_first)
        def _():
            fetched = []
            for i, (ref, (at, size)) in enumerate(zip(feeds, places)):
                fetched.append(pltpu.make_async_copy(
                    ref.at[t - 1, :size], context.at[at:at + size], sems.at[2 * i]))
                fetched.append(pltpu.make_async_copy(
                    ref.at[t - 1, size:], marks.at[i], sems.at[2 * i + 1]))
            for copy in fetched:
                copy.start()
            for copy in fetched:
                copy.wait()

        pl.when(jnp.logical_not(is_first))(relayed)
    else:
        relayed()

    wide = 2 * HALO + count
    seen = sum(marks[i, 0:1, :wide].astype(jnp.float32) for i in range(3))
    normed[...] = _normed(context[...].astype(jnp.float32), gain_ref[...])

    def columns(a, lo, hi):
        return weights[a, :, :, :, lo:hi].reshape(-1, hi - lo)

    wait(0)
    for n in range(3):
        qkv[:, n * INNER:(n + 1) * INNER] = _dot(
            normed[...], columns(0, n * INNER, (n + 1) * INNER), ((1,), (0,))).astype(jnp.bfloat16)

    row = lax.broadcasted_iota(jnp.int32, (count, length), 0)
    col = lax.broadcasted_iota(jnp.int32, (count, length), 1) - HALO
    allowed = (jnp.abs(col - row) <= HALO) & ((seen > 0.5) | (col == row))
    barred = jnp.where(allowed, 0.0, 1.0)
    barred = jnp.concatenate([barred, barred], axis=0) > 0.5
    lane = lax.broadcasted_iota(jnp.int32, (count, 2 * HEAD), 1)
    parts = []
    for pair in range(HEADS // 2):
        lo = pair * 2 * HEAD
        q = qkv[HALO:HALO + count, lo:lo + 2 * HEAD]
        k = qkv[:, INNER + lo:INNER + lo + 2 * HEAD]
        v = qkv[:, 2 * INNER + lo:2 * INNER + lo + 2 * HEAD]
        zero = jnp.zeros_like(q)
        both = jnp.concatenate(
            [jnp.where(lane < HEAD, q, zero), jnp.where(lane < HEAD, zero, q)], axis=0)
        scores = _dot(both, k, ((1,), (1,))) * HEAD ** (-0.5)
        scores = jnp.where(barred, jnp.float32(-1e30), scores)
        highest = jnp.max(scores, axis=-1, keepdims=True)
        exps = jnp.exp(scores - highest)
        totals = jnp.sum(exps, axis=-1, keepdims=True)
        shares = (exps / totals).astype(jnp.bfloat16)
        mixed = _dot(shares, v, ((1,), (0,)))
        parts.append(jnp.where(lane < HEAD, mixed[:count], mixed[count:]).astype(jnp.bfloat16))
    attended = context[HALO:HALO + count].astype(jnp.float32) + _dot(
        jnp.concatenate(parts, axis=1), columns(0, 3 * INNER, 4 * INNER), ((1,), (1,)))
    attended = attended.astype(jnp.bfloat16)
    context[:count] = attended
    normed[:count] = _normed(attended.astype(jnp.float32), gain_mlp_ref[...])
    wait(1)
    for lo in range(0, hidden.shape[1], TILE):
        up = _dot(normed[:count], columns(1, lo, lo + TILE), ((1,), (0,)))
        up = 0.5 * up * (1.0 + lax.erf(up * (0.5 ** 0.5)))
        hidden[:, lo:lo + TILE] = up.astype(jnp.bfloat16)
    wait(2)
    for g in range(0, weights.shape[1], 2):
        w = weights[2, g:g + 2]
        w = w.reshape(-1, w.shape[-1])
        size = w.shape[0]
        lo = g * size // 2
        result = (context[:count, lo:lo + size].astype(jnp.float32) + _dot(
            hidden[...], w, ((1,), (1,)))).astype(jnp.bfloat16)
        out_ref[:, lo:lo + size] = result
        if t < TICKS - 1:
            main_out[:count, lo:lo + size] = result
            after_out[:HALO, lo:lo + size] = result[:HALO]
            before_out[:HALO, lo:lo + size] = result[count - HALO:]
    if t < TICKS - 1:
        at = lax.broadcasted_iota(jnp.int32, (MARKS, count), 1)
        left = jnp.broadcast_to(seen[:, :count], (MARKS, count))
        right = jnp.broadcast_to(seen[:, count:], (MARKS, count))
        none = jnp.zeros((MARKS, count), jnp.float32)
        left = jnp.where(at >= HALO, left, none)
        right = jnp.where(at < HALO, right, none)
        for ref, lows, highs in (
            (before_out, right, none), (main_out, left, right), (after_out, none, left)
        ):
            size = ref.shape[0] - MARKS
            ref[size:] = jnp.zeros((MARKS, ref.shape[1]), ref.dtype)
            ref[size:, :count] = lows.astype(ref.dtype)
            ref[size:, count:2 * count] = highs.astype(ref.dtype)


def tick(t, flags, gain, gain_mlp, payload, feeds, weights, pieces, spots):
    width = payload[0].shape[1]
    count = payload[1].shape[0] - MARKS
    length = count + 2 * HALO
    hidden = weights.shape[-1]
    vmem = pl.BlockSpec(memory_space=pltpu.VMEM)
    anyw = pl.BlockSpec(memory_space=pl.ANY)
    small = ((HALO, count, HALO) if t < TICKS - 1 else (0, 0, 0))
    outs = [jax.ShapeDtypeStruct((count, width), jnp.bfloat16)]
    outs += [jax.ShapeDtypeStruct((size + MARKS, width), jnp.bfloat16) for size in small]
    if t == 0:
        outs.append(jax.ShapeDtypeStruct(weights.shape, jnp.bfloat16))
        operands = list(payload) + list(pieces) + [weights]
        specs = [vmem] * 3 + [anyw] * len(pieces) + [vmem]
    else:
        operands = list(payload) + list(feeds) + [weights]
        specs = [vmem] * 3 + [anyw] * 3 + [vmem]
    return pl.pallas_call(
        functools.partial(tick_kernel, t, spots),
        out_shape=tuple(outs),
        in_specs=[pl.BlockSpec(memory_space=pltpu.SMEM), vmem, vmem] + specs,
        out_specs=tuple([vmem] * len(outs)),
        input_output_aliases={6 + len(pieces): 4} if t == 0 else {},
        scratch_shapes=[
            pltpu.VMEM((length, 3 * INNER), jnp.bfloat16),
            pltpu.VMEM((length, width), jnp.bfloat16),
            pltpu.VMEM((3, MARKS, width), jnp.bfloat16),
            pltpu.VMEM((length, width), jnp.bfloat16),
            pltpu.VMEM((count, hidden), jnp.bfloat16),
            pltpu.SemaphoreType.DMA((6,)),
            pltpu.SemaphoreType.DMA((3, max(1, sum(len(p) for p in spots)))),
        ],
        compiler_params=pltpu.CompilerParams(vmem_limit_bytes=22 * 1024 * 1024),
        name=f"tick{t}",
    )(flags, gain, gain_mlp, *operands)


def gather_rows(own):
    rows = lax.axis_size("y")
    far = rows // 2

    def swapped(value, mask):
        return lax.ppermute(value, "z", [(z, z ^ mask) for z in range(ZL)])

    def moved(value, delta):
        return lax.ppermute(value, "y", [(y, (y + delta) % rows) for y in range(rows)])

    def ring(chunks, steps):
        for step in steps:
            chunks[-step] = moved(chunks[1 - step], 1)
            chunks[step] = moved(chunks[step - 1], -1)

    near = {0: own}
    second = swapped(own, 2)
    ring(near, (1,))
    delayed, _ = lax.optimization_barrier((own, (near[-1], near[1])))
    third = swapped(delayed, 3)
    ring(near, range(2, far))
    near[far] = moved(near[1 - far], 1)
    second, third, _ = lax.optimization_barrier((second, third, (near[-2], near[2])))
    others = {0: jnp.stack([second, third])}
    ring(others, range(1, far))
    others[far] = moved(others[far - 1], -1)
    partner = {}
    for group in ((0, -1, 1), (-2, 2), (-3, 3, far)):
        partner[group] = swapped(jnp.stack([near[delta] for delta in group]), 1)
    stages = []
    for mine, theirs, groups in (
        (tuple(near), (0, -1, 1), ((0, -1, 1),)),
        ((), (-2, 2), ((-2, 2),)),
        ((), (-3, 3, far), ((-3, 3, far),)),
    ):
        pieces = [near[d] for d in mine] + [others[d] for d in theirs] + [partner[g] for g in groups]
        spots = [((d, 0),) for d in mine] + [((d, 2), (d, 3)) for d in theirs]
        spots += [tuple((d, 1) for d in g) for g in groups]
        stages.append((pieces, spots))
    return stages, near, others


def body(
    fresh_tokens,
    fresh_mask,
    curve_order,
    held_state,
    held_mask,
    norm_gains,
    projections,
    mlp_gains,
    mlp_up,
    mlp_down,
):
    sections, seqs = lax.axis_size("section"), lax.axis_size(SEQ)
    is_first = lax.axis_index("section") == 0
    count, width = held_state.shape[1:]
    depth = projections.shape[2]

    own = jnp.stack([
        projections[0].transpose(1, 0, 2).reshape(depth, 4 * INNER),
        mlp_up[0],
        mlp_down[0],
    ])
    stages, near, others = gather_rows(own)
    flags = jnp.stack([
        is_first.astype(jnp.int32),
        lax.axis_index("y").astype(jnp.int32),
        lax.axis_index("z").astype(jnp.int32),
    ])
    shape = (3, seqs // ZL, ZL, depth, own.shape[2])

    def payloads(tokens, mask, names):
        mask = mask.astype(jnp.bfloat16)

        def marked(part, seen, at):
            line = jnp.pad(seen, ((0, 0), (at, width - at - seen.shape[1])))[:, None]
            line = jnp.broadcast_to(line, (part.shape[0], MARKS, width))
            return jnp.concatenate([part, line], axis=1)

        up = [(i, i + 1) for i in range(seqs - 1)]
        down = [(i + 1, i) for i in range(seqs - 1)]
        main = marked(tokens, mask, HALO)
        before = lax.ppermute(marked(tokens[:, count - HALO:], mask[:, count - HALO:], 0), names, up)
        after = lax.ppermute(marked(tokens[:, :HALO], mask[:, :HALO], HALO + count), names, down)
        return before, main, after

    _, held_state, held_mask = lax.optimization_barrier((others[-1], held_state, held_mask))
    payload = [part[0] for part in payloads(held_state, held_mask, SEQ)]

    _, fresh_tokens, fresh_mask, curve_order = lax.optimization_barrier(
        (near[-3], fresh_tokens, fresh_mask, curve_order))
    local_order = curve_order - lax.axis_index(SEQ) * count
    serial_tokens = jax.vmap(lambda source, indices: jnp.take(source, indices, axis=0))(
        fresh_tokens, local_order
    )
    serial_mask = jnp.take_along_axis(fresh_mask, local_order, axis=1)
    feeds = payloads(serial_tokens, serial_mask, ("section",) + SEQ)

    def relay(shift):
        return [
            (s * seqs + j, (s + 1) * seqs + j + shift)
            for s in range(sections - 1) for j in range(seqs) if 0 <= j + shift < seqs
        ]

    every = ("section",) + SEQ
    results = []
    weights = None
    for i, (pieces, spots) in enumerate(stages[:-1]):
        weights = place(flags, weights, pieces, spots, shape, f"place{i}")
    for t in range(TICKS):
        pieces, spots = stages[-1] if t == 0 else ((), ())
        outs = tick(t, flags, norm_gains, mlp_gains, payload, feeds, weights, pieces, spots)
        results.append(outs[0])
        if t == 0:
            weights = outs[4]
        if t < TICKS - 1:
            before, main, after = outs[1:4]
            payload = (
                lax.ppermute(before, every, relay(1)),
                lax.ppermute(main, every, relay(0)),
                lax.ppermute(after, every, relay(-1)),
            )
    return jnp.stack(results)[:, None]


def solution(mesh):
    sections, seqs = mesh.shape["section"], mesh.shape["seq"]
    split = Mesh(mesh.devices.reshape(sections, seqs // ZL, ZL), ("section",) + SEQ)
    return jax.shard_map(
        body,
        mesh=split,
        in_specs=(
            P(None, SEQ, None),
            P(None, SEQ),
            P(None, SEQ),
            P("section", SEQ, None),
            P("section", SEQ),
            P("section", None),
            P("section", None, SEQ, None),
            P("section", None),
            P("section", SEQ, None),
            P("section", SEQ, None),
        ),
        out_specs=P(None, "section", SEQ, None),
        check_vma=False,
    )
```

```python
import functools

import jax
import jax.numpy as jnp
from jax import lax
from jax.experimental import pallas as pl
from jax.experimental.pallas import tpu as pltpu
from jax.sharding import Mesh, PartitionSpec as P

HEADS = 8
HEAD = 64
INNER = 512
HALO = 64
TICKS = 4
ZL = 4
TILE = 512
MARKS = 16
SEQ = ("y", "z")


def _normed(values, gain):
    average = jnp.mean(values, axis=-1, keepdims=True)
    centered = values - average
    spread_sq = jnp.mean(centered * centered, axis=-1, keepdims=True)
    return (centered * lax.rsqrt(spread_sq + 1e-05) * gain).astype(jnp.bfloat16)


def _dot(a, b, dims):
    return lax.dot_general(a, b, (dims, ((), ())), preferred_element_type=jnp.float32)


def chunk_copies(flags_ref, weights, pieces, spots, sems):
    my_y, my_z = flags_ref[1], flags_ref[2]
    rows = weights.shape[1]
    flipped = my_z + 1 - 2 * lax.rem(my_z, 2)
    columns_at = (my_z, flipped, lax.rem(my_z + 2, ZL), ZL - 1 - my_z)
    found, slot = [], 0
    for piece, places in zip(pieces, spots):
        for i, (delta, mask) in enumerate(places):
            y = lax.rem(my_y + (delta + rows), rows)
            chunk = piece if len(piece.shape) == 3 else piece.at[i]
            found.append(pltpu.make_async_copy(
                chunk, weights.at[:, y, columns_at[mask]], sems.at[slot]))
            slot += 1
    return found


def place_kernel(spots, fresh, flags_ref, *refs):
    weights, sems = refs[-2:]
    pieces = refs[:-2] if fresh else refs[1:-2]
    copies = chunk_copies(flags_ref, weights, pieces, spots, sems)
    for copy in copies:
        copy.start()
    for copy in copies:
        copy.wait()


def place(flags, weights, pieces, spots, shape, name):
    fresh = weights is None
    anyw = pl.BlockSpec(memory_space=pl.ANY)
    held = [] if fresh else [weights]
    chunks = sum(len(p) for p in spots)
    moved_bytes = 2 * chunks * shape[0] * shape[3] * shape[4] * 2
    return pl.pallas_call(
        functools.partial(place_kernel, spots, fresh),
        out_shape=jax.ShapeDtypeStruct(shape, jnp.bfloat16),
        in_specs=[pl.BlockSpec(memory_space=pltpu.SMEM)] + [anyw] * (len(held) + len(pieces)),
        out_specs=anyw,
        input_output_aliases={} if fresh else {1: 0},
        scratch_shapes=[pltpu.SemaphoreType.DMA((chunks,))],
        compiler_params=pltpu.CompilerParams(vmem_limit_bytes=16 * 1024 * 1024),
        cost_estimate=pl.CostEstimate(flops=0, bytes_accessed=moved_bytes, transcendentals=0),
        name=name,
    )(flags, *held, *pieces)


def tick_kernel(t, flags_ref, gain_ref, gain_mlp_ref, *refs):
    broad = t % 2 == 0
    size = 3 if broad else 1
    relayed, refs = refs[:size], refs[size:]
    feeds = ()
    if t > 0:
        feeds, refs = refs[:3], refs[3:]
    weights, out_ref, refs = refs[0], refs[1], refs[2:]
    if t < TICKS - 1:
        onward_ref, refs = refs[0], refs[1:]
    qkv, context, marks, seen, normed, hidden, sems = refs
    count = out_ref.shape[0]
    edge = 2 * HALO if broad else HALO
    length = count + 2 * edge
    kept = length - 2 * HALO

    def shifted(lines, width):
        return pltpu.roll(lines, lines.shape[1] - HALO, 1)[:, :width]

    def joined():
        return jnp.concatenate(
            [marks[i, :, :count].astype(jnp.float32) for i in range(3)], axis=1)

    def arrived():
        if broad:
            for i, ref in enumerate(relayed):
                context[i * count:(i + 1) * count] = ref[:count]
                marks[i] = ref[count:]
            seen[...] = joined()
        else:
            context[:length] = relayed[0][:length]
            seen[:, :length] = relayed[0][length:, :length].astype(jnp.float32)

    if feeds:
        @pl.when(flags_ref[0] == 1)
        def _():
            before_ref, main_ref, after_ref = feeds
            at = (0, HALO, HALO + count)[t - 1]
            tail = before_ref.shape[0] - MARKS
            moves = (
                (before_ref.at[at:at + edge], context.at[:edge]),
                (main_ref.at[t - 1, :count], context.at[edge:edge + count]),
                (after_ref.at[at:at + edge], context.at[edge + count:length]),
                (before_ref.at[tail:], marks.at[0]),
                (main_ref.at[t - 1, count:], marks.at[1]),
                (after_ref.at[tail:], marks.at[2]),
            )
            fetched = [
                pltpu.make_async_copy(source, target, sems.at[i])
                for i, (source, target) in enumerate(moves)
            ]
            for copy in fetched:
                copy.start()
            for copy in fetched:
                copy.wait()
            if broad:
                seen[...] = joined()
            else:
                seen[:, :length] = shifted(joined(), length)

        pl.when(flags_ref[0] != 1)(arrived)
    else:
        arrived()

    pick = max(t - 1, 0)
    line = seen[pick:pick + 1, :length]
    for lo in range(0, length, count):
        normed[lo:lo + count] = _normed(context[lo:lo + count].astype(jnp.float32), gain_ref[...])

    def columns(a, lo, hi):
        return weights[a, :, :, :, lo:hi].reshape(-1, hi - lo)

    for n in range(3):
        qkv[:length, n * INNER:(n + 1) * INNER] = _dot(
            normed[:length], columns(0, n * INNER, (n + 1) * INNER), ((1,), (0,))
        ).astype(jnp.bfloat16)

    reach = count + 2 * HALO
    row = lax.broadcasted_iota(jnp.int32, (count, reach), 0)
    col = lax.broadcasted_iota(jnp.int32, (count, reach), 1) - HALO
    lane = lax.broadcasted_iota(jnp.int32, (count, 2 * HEAD), 1)
    for lo in range(0, kept, count):
        allowed = (jnp.abs(col - row) <= HALO) & ((line[:, lo:lo + reach] > 0.5) | (col == row))
        barred = jnp.where(allowed, 0.0, 1.0)
        barred = jnp.concatenate([barred, barred], axis=0) > 0.5
        for pair in range(HEADS // 2):
            at = pair * 2 * HEAD
            q = qkv[lo + HALO:lo + HALO + count, at:at + 2 * HEAD]
            k = qkv[lo:lo + reach, INNER + at:INNER + at + 2 * HEAD]
            v = qkv[lo:lo + reach, 2 * INNER + at:2 * INNER + at + 2 * HEAD]
            zero = jnp.zeros_like(q)
            both = jnp.concatenate(
                [jnp.where(lane < HEAD, q, zero), jnp.where(lane < HEAD, zero, q)], axis=0)
            scores = _dot(both, k, ((1,), (1,))) * HEAD ** (-0.5)
            scores = jnp.where(barred, jnp.float32(-1e30), scores)
            highest = jnp.max(scores, axis=-1, keepdims=True)
            exps = jnp.exp(scores - highest)
            totals = jnp.sum(exps, axis=-1, keepdims=True)
            shares = (exps / totals).astype(jnp.bfloat16)
            mixed = _dot(shares, v, ((1,), (0,)))
            hidden[lo:lo + count, at:at + 2 * HEAD] = jnp.where(
                lane < HEAD, mixed[:count], mixed[count:]).astype(jnp.bfloat16)
    attended = context[HALO:HALO + kept].astype(jnp.float32) + _dot(
        hidden[:kept, :INNER], columns(0, 3 * INNER, 4 * INNER), ((1,), (1,)))
    attended = attended.astype(jnp.bfloat16)
    context[:kept] = attended
    normed[:kept] = _normed(attended.astype(jnp.float32), gain_mlp_ref[...])
    for lo in range(0, hidden.shape[1], TILE):
        up = _dot(normed[:kept], columns(1, lo, lo + TILE), ((1,), (0,)))
        up = 0.5 * up * (1.0 + lax.erf(up * (0.5 ** 0.5)))
        hidden[:kept, lo:lo + TILE] = up.astype(jnp.bfloat16)
    first = edge - HALO
    for g in range(0, weights.shape[1], 2):
        w = weights[2, g:g + 2]
        w = w.reshape(-1, w.shape[-1])
        size = w.shape[0]
        lo = g * size // 2
        result = (context[:kept, lo:lo + size].astype(jnp.float32) + _dot(
            hidden[:kept], w, ((1,), (1,)))).astype(jnp.bfloat16)
        out_ref[:, lo:lo + size] = result[first:first + count]
        if t < TICKS - 1:
            onward_ref[:kept, lo:lo + size] = result
    if t < TICKS - 1:
        onward_ref[kept:] = jnp.zeros((MARKS, onward_ref.shape[1]), onward_ref.dtype)
        lines = jnp.broadcast_to(line, (MARKS, length))
        onward_ref[kept:, :kept] = shifted(lines, kept).astype(onward_ref.dtype)


def tick(t, flags, gain, gain_mlp, payload, feeds, weights):
    width, hidden = payload[0].shape[1], weights.shape[-1]
    broad = t % 2 == 0
    count = payload[0].shape[0] - MARKS - (0 if broad else 2 * HALO)
    length = count + (4 if broad else 2) * HALO
    vmem = pl.BlockSpec(memory_space=pltpu.VMEM)
    anyw = pl.BlockSpec(memory_space=pl.ANY)
    outs = [jax.ShapeDtypeStruct((count, width), jnp.bfloat16)]
    if t < TICKS - 1:
        outs.append(jax.ShapeDtypeStruct((length - 2 * HALO + MARKS, width), jnp.bfloat16))
    operands = list(payload) + list(feeds if t > 0 else ()) + [weights]
    specs = [vmem] * len(payload) + [anyw] * (len(operands) - len(payload) - 1) + [vmem]
    return pl.pallas_call(
        functools.partial(tick_kernel, t),
        out_shape=tuple(outs),
        in_specs=[pl.BlockSpec(memory_space=pltpu.SMEM), vmem, vmem] + specs,
        out_specs=tuple([vmem] * len(outs)),
        scratch_shapes=[
            pltpu.VMEM((length, 3 * INNER), jnp.bfloat16),
            pltpu.VMEM((length, width), jnp.bfloat16),
            pltpu.VMEM((3, MARKS, width), jnp.bfloat16),
            pltpu.VMEM((MARKS, length if broad else count + 4 * HALO), jnp.float32),
            pltpu.VMEM((length, width), jnp.bfloat16),
            pltpu.VMEM((length - 2 * HALO, hidden), jnp.bfloat16),
            pltpu.SemaphoreType.DMA((6,)),
        ],
        compiler_params=pltpu.CompilerParams(vmem_limit_bytes=26 * 1024 * 1024),
        name=f"tick{t}",
    )(flags, gain, gain_mlp, *operands)


def gather_rows(own):
    rows = lax.axis_size("y")
    far = rows // 2

    def swapped(value, mask):
        return lax.ppermute(value, "z", [(z, z ^ mask) for z in range(ZL)])

    def moved(value, delta):
        return lax.ppermute(value, "y", [(y, (y + delta) % rows) for y in range(rows)])

    def ring(chunks, steps):
        for step in steps:
            chunks[-step] = moved(chunks[1 - step], 1)
            chunks[step] = moved(chunks[step - 1], -1)

    near, others = {0: own}, {}
    ring(near, (1,))
    others[0] = jnp.stack([swapped(own, 2), swapped(own, 3)])
    ring(near, range(2, far))
    near[far] = moved(near[1 - far], 1)
    ring(others, range(1, far))
    others[far] = moved(others[far - 1], -1)
    halves = ((0, -1, 1, -2, 2), (-3, 3, far))
    rest = jnp.stack([near[delta] for delta in halves[1]])
    rest, _ = lax.optimization_barrier((rest, others[-2]))
    partner = {
        halves[0]: swapped(jnp.stack([near[delta] for delta in halves[0]]), 1),
        halves[1]: swapped(rest, 1),
    }
    stages = []
    for mine, theirs, groups in (
        (tuple(near), (0, -1, 1), halves[:1]),
        ((), (-2, 2), ()),
        ((), (-3, 3, far), halves[1:]),
    ):
        pieces = [near[d] for d in mine] + [others[d] for d in theirs] + [partner[g] for g in groups]
        spots = [((d, 0),) for d in mine] + [((d, 2), (d, 3)) for d in theirs]
        spots += [tuple((d, 1) for d in g) for g in groups]
        stages.append((pieces, spots))
    return stages, near, others


def body(
    fresh_tokens,
    fresh_mask,
    curve_order,
    held_state,
    held_mask,
    norm_gains,
    projections,
    mlp_gains,
    mlp_up,
    mlp_down,
):
    sections, seqs = lax.axis_size("section"), lax.axis_size(SEQ)
    is_first = lax.axis_index("section") == 0
    count, width = held_state.shape[1:]
    depth = projections.shape[2]

    own = jnp.stack([
        projections[0].transpose(1, 0, 2).reshape(depth, 4 * INNER),
        mlp_up[0],
        mlp_down[0],
    ])
    stages, near, others = gather_rows(own)
    flags = jnp.stack([
        is_first.astype(jnp.int32),
        lax.axis_index("y").astype(jnp.int32),
        lax.axis_index("z").astype(jnp.int32),
    ])
    shape = (3, seqs // ZL, ZL, depth, own.shape[2])

    up = [(i, i + 1) for i in range(seqs - 1)]
    down = [(i + 1, i) for i in range(seqs - 1)]

    def marked(mask):
        lines = jnp.pad(mask.astype(jnp.bfloat16), ((0, 0), (0, width - count)))[:, None]
        return jnp.broadcast_to(lines, (mask.shape[0], MARKS, width))

    _, held_state, held_mask = lax.optimization_barrier((others[-1], held_state, held_mask))
    main = jnp.concatenate([held_state, marked(held_mask)], axis=1)[0]
    payload = (lax.ppermute(main, SEQ, up), main, lax.ppermute(main, SEQ, down))

    local_order = curve_order - lax.axis_index(SEQ) * count
    serial_tokens = jax.vmap(lambda source, indices: jnp.take(source, indices, axis=0))(
        fresh_tokens, local_order
    )
    serial_mask = jnp.take_along_axis(fresh_mask, local_order, axis=1)
    every = ("section",) + SEQ
    lines = jnp.pad(
        serial_mask.astype(jnp.bfloat16), ((0, MARKS - TICKS + 1), (0, width - count)))
    lasts = jnp.concatenate([serial_tokens[0, count - HALO:], serial_tokens[1],
                             serial_tokens[2, count - HALO:], lines])
    firsts = jnp.concatenate([serial_tokens[0, :HALO], serial_tokens[1],
                              serial_tokens[2, :HALO], lines])
    lasts, firsts, _ = lax.optimization_barrier((lasts, firsts, others[-1]))
    feeds = (
        lax.ppermute(lasts, every, up),
        jnp.concatenate([serial_tokens, marked(serial_mask)], axis=1),
        lax.ppermute(firsts, every, down),
    )

    def relay(value, shift):
        return lax.ppermute(value, every, [
            (s * seqs + j, (s + 1) * seqs + j + shift)
            for s in range(sections - 1) for j in range(seqs) if 0 <= j + shift < seqs
        ])

    results = []
    weights = None
    for i, (pieces, spots) in enumerate(stages):
        weights = place(flags, weights, pieces, spots, shape, f"place{i}")
    for t in range(TICKS):
        outs = tick(t, flags, norm_gains, mlp_gains, payload, feeds, weights)
        results.append(outs[0])
        if t < TICKS - 1:
            shifts = (0,) if t % 2 == 0 else (1, 0, -1)
            payload = tuple(relay(outs[1], shift) for shift in shifts)
    return jnp.stack(results)[:, None]


def solution(mesh):
    sections, seqs = mesh.shape["section"], mesh.shape["seq"]
    split = Mesh(mesh.devices.reshape(sections, seqs // ZL, ZL), ("section",) + SEQ)
    return jax.shard_map(
        body,
        mesh=split,
        in_specs=(
            P(None, SEQ, None),
            P(None, SEQ),
            P(None, SEQ),
            P("section", SEQ, None),
            P("section", SEQ),
            P("section", None),
            P("section", None, SEQ, None),
            P("section", None),
            P("section", SEQ, None),
            P("section", SEQ, None),
        ),
        out_specs=P(None, "section", SEQ, None),
        check_vma=False,
    )
```

```python
import functools

import jax
import jax.numpy as jnp
from jax import lax
from jax.experimental import pallas as pl
from jax.experimental.pallas import tpu as pltpu
from jax.sharding import Mesh, PartitionSpec as P

HEADS = 8
HEAD = 64
INNER = 512
HALO = 64
TICKS = 4
ZL = 4
TILE = 512
MARKS = 16
SEQ = ("y", "z")


def _normed(values, gain):
    average = jnp.mean(values, axis=-1, keepdims=True)
    centered = values - average
    spread_sq = jnp.mean(centered * centered, axis=-1, keepdims=True)
    return (centered * lax.rsqrt(spread_sq + 1e-05) * gain).astype(jnp.bfloat16)


def _dot(a, b, dims):
    return lax.dot_general(a, b, (dims, ((), ())), preferred_element_type=jnp.float32)


def chunk_copies(flags_ref, weights, pieces, spots, sems):
    my_y, my_z = flags_ref[1], flags_ref[2]
    rows = weights.shape[1]
    flipped = my_z + 1 - 2 * lax.rem(my_z, 2)
    columns_at = (my_z, flipped, lax.rem(my_z + 2, ZL), ZL - 1 - my_z)
    found, slot = [], 0
    for piece, places in zip(pieces, spots):
        for i, (delta, mask) in enumerate(places):
            y = lax.rem(my_y + (delta + rows), rows)
            chunk = piece if len(piece.shape) == 3 else piece.at[i]
            found.append(pltpu.make_async_copy(
                chunk, weights.at[:, y, columns_at[mask]], sems.at[slot]))
            slot += 1
    return found


def place_kernel(spots, fresh, flags_ref, *refs):
    weights, sems = refs[-2:]
    pieces = refs[:-2] if fresh else refs[1:-2]
    copies = chunk_copies(flags_ref, weights, pieces, spots, sems)
    for copy in copies:
        copy.start()
    for copy in copies:
        copy.wait()


def place(flags, weights, pieces, spots, shape, name):
    fresh = weights is None
    anyw = pl.BlockSpec(memory_space=pl.ANY)
    held = [] if fresh else [weights]
    chunks = sum(len(p) for p in spots)
    moved_bytes = 2 * chunks * shape[0] * shape[3] * shape[4] * 2
    return pl.pallas_call(
        functools.partial(place_kernel, spots, fresh),
        out_shape=jax.ShapeDtypeStruct(shape, jnp.bfloat16),
        in_specs=[pl.BlockSpec(memory_space=pltpu.SMEM)] + [anyw] * (len(held) + len(pieces)),
        out_specs=anyw,
        input_output_aliases={} if fresh else {1: 0},
        scratch_shapes=[pltpu.SemaphoreType.DMA((chunks,))],
        compiler_params=pltpu.CompilerParams(vmem_limit_bytes=16 * 1024 * 1024),
        cost_estimate=pl.CostEstimate(flops=0, bytes_accessed=moved_bytes, transcendentals=0),
        name=name,
    )(flags, *held, *pieces)


def tick_kernel(t, flags_ref, gain_ref, gain_mlp_ref, *refs):
    broad = t % 2 == 0
    size = 3 if broad else 1
    relayed, refs = refs[:size], refs[size:]
    feeds = ()
    if t > 0:
        feeds, refs = refs[:3], refs[3:]
    weights, out_ref, refs = refs[0], refs[1], refs[2:]
    if t < TICKS - 1:
        onward_ref, refs = refs[0], refs[1:]
    qkv, context, marks, seen, normed, hidden, sems = refs
    count = out_ref.shape[0]
    edge = 2 * HALO if broad else HALO
    length = count + 2 * edge
    kept = length - 2 * HALO

    def shifted(lines, width):
        return pltpu.roll(lines, lines.shape[1] - HALO, 1)[:, :width]

    def joined():
        return jnp.concatenate(
            [marks[i, :, :count].astype(jnp.float32) for i in range(3)], axis=1)

    def arrived():
        if broad:
            for i, ref in enumerate(relayed):
                context[i * count:(i + 1) * count] = ref[:count]
                marks[i] = ref[count:]
            seen[...] = joined()
        else:
            context[:length] = relayed[0][:length]
            seen[:, :length] = relayed[0][length:, :length].astype(jnp.float32)

    if feeds:
        @pl.when(flags_ref[0] == 1)
        def _():
            before_ref, main_ref, after_ref = feeds
            at = (0, HALO, HALO + count)[t - 1]
            tail = before_ref.shape[0] - MARKS
            moves = (
                (before_ref.at[at:at + edge], context.at[:edge]),
                (main_ref.at[t - 1, :count], context.at[edge:edge + count]),
                (after_ref.at[at:at + edge], context.at[edge + count:length]),
                (before_ref.at[tail:], marks.at[0]),
                (main_ref.at[t - 1, count:], marks.at[1]),
                (after_ref.at[tail:], marks.at[2]),
            )
            fetched = [
                pltpu.make_async_copy(source, target, sems.at[i])
                for i, (source, target) in enumerate(moves)
            ]
            for copy in fetched:
                copy.start()
            for copy in fetched:
                copy.wait()
            if broad:
                seen[...] = joined()
            else:
                seen[:, :length] = shifted(joined(), length)

        pl.when(flags_ref[0] != 1)(arrived)
    else:
        arrived()

    pick = max(t - 1, 0)
    line = seen[pick:pick + 1, :length]
    for lo in range(0, length, count):
        normed[lo:lo + count] = _normed(context[lo:lo + count].astype(jnp.float32), gain_ref[...])

    def columns(a, lo, hi):
        return weights[a, :, :, :, lo:hi].reshape(-1, hi - lo)

    for n in range(3):
        qkv[:length, n * INNER:(n + 1) * INNER] = _dot(
            normed[:length], columns(0, n * INNER, (n + 1) * INNER), ((1,), (0,))
        ).astype(jnp.bfloat16)

    reach = count + 2 * HALO
    row = lax.broadcasted_iota(jnp.int32, (count, reach), 0)
    col = lax.broadcasted_iota(jnp.int32, (count, reach), 1) - HALO
    lane = lax.broadcasted_iota(jnp.int32, (count, 2 * HEAD), 1)
    for lo in range(0, kept, count):
        allowed = (jnp.abs(col - row) <= HALO) & ((line[:, lo:lo + reach] > 0.5) | (col == row))
        barred = jnp.where(allowed, 0.0, 1.0)
        barred = jnp.concatenate([barred, barred], axis=0) > 0.5
        for pair in range(HEADS // 2):
            at = pair * 2 * HEAD
            q = qkv[lo + HALO:lo + HALO + count, at:at + 2 * HEAD]
            k = qkv[lo:lo + reach, INNER + at:INNER + at + 2 * HEAD]
            v = qkv[lo:lo + reach, 2 * INNER + at:2 * INNER + at + 2 * HEAD]
            zero = jnp.zeros_like(q)
            both = jnp.concatenate(
                [jnp.where(lane < HEAD, q, zero), jnp.where(lane < HEAD, zero, q)], axis=0)
            scores = _dot(both, k, ((1,), (1,))) * HEAD ** (-0.5)
            scores = jnp.where(barred, jnp.float32(-1e30), scores)
            highest = jnp.max(scores, axis=-1, keepdims=True)
            exps = jnp.exp(scores - highest)
            totals = jnp.sum(exps, axis=-1, keepdims=True)
            shares = (exps / totals).astype(jnp.bfloat16)
            mixed = _dot(shares, v, ((1,), (0,)))
            hidden[lo:lo + count, at:at + 2 * HEAD] = jnp.where(
                lane < HEAD, mixed[:count], mixed[count:]).astype(jnp.bfloat16)
    attended = context[HALO:HALO + kept].astype(jnp.float32) + _dot(
        hidden[:kept, :INNER], columns(0, 3 * INNER, 4 * INNER), ((1,), (1,)))
    attended = attended.astype(jnp.bfloat16)
    context[:kept] = attended
    normed[:kept] = _normed(attended.astype(jnp.float32), gain_mlp_ref[...])
    for lo in range(0, hidden.shape[1], TILE):
        up = _dot(normed[:kept], columns(1, lo, lo + TILE), ((1,), (0,)))
        up = 0.5 * up * (1.0 + lax.erf(up * (0.5 ** 0.5)))
        hidden[:kept, lo:lo + TILE] = up.astype(jnp.bfloat16)
    first = edge - HALO
    for g in range(0, weights.shape[1], 2):
        w = weights[2, g:g + 2]
        w = w.reshape(-1, w.shape[-1])
        size = w.shape[0]
        lo = g * size // 2
        result = (context[:kept, lo:lo + size].astype(jnp.float32) + _dot(
            hidden[:kept], w, ((1,), (1,)))).astype(jnp.bfloat16)
        out_ref[:, lo:lo + size] = result[first:first + count]
        if t < TICKS - 1:
            onward_ref[:kept, lo:lo + size] = result
    if t < TICKS - 1:
        onward_ref[kept:] = jnp.zeros((MARKS, onward_ref.shape[1]), onward_ref.dtype)
        lines = jnp.broadcast_to(line, (MARKS, length))
        onward_ref[kept:, :kept] = shifted(lines, kept).astype(onward_ref.dtype)


def tick(t, flags, gain, gain_mlp, payload, feeds, weights):
    width, hidden = payload[0].shape[1], weights.shape[-1]
    broad = t % 2 == 0
    count = payload[0].shape[0] - MARKS - (0 if broad else 2 * HALO)
    length = count + (4 if broad else 2) * HALO
    vmem = pl.BlockSpec(memory_space=pltpu.VMEM)
    anyw = pl.BlockSpec(memory_space=pl.ANY)
    outs = [jax.ShapeDtypeStruct((count, width), jnp.bfloat16)]
    if t < TICKS - 1:
        outs.append(jax.ShapeDtypeStruct((length - 2 * HALO + MARKS, width), jnp.bfloat16))
    operands = list(payload) + list(feeds if t > 0 else ()) + [weights]
    specs = [vmem] * len(payload) + [anyw] * (len(operands) - len(payload) - 1) + [vmem]
    return pl.pallas_call(
        functools.partial(tick_kernel, t),
        out_shape=tuple(outs),
        in_specs=[pl.BlockSpec(memory_space=pltpu.SMEM), vmem, vmem] + specs,
        out_specs=tuple([vmem] * len(outs)),
        scratch_shapes=[
            pltpu.VMEM((length, 3 * INNER), jnp.bfloat16),
            pltpu.VMEM((length, width), jnp.bfloat16),
            pltpu.VMEM((3, MARKS, width), jnp.bfloat16),
            pltpu.VMEM((MARKS, length if broad else count + 4 * HALO), jnp.float32),
            pltpu.VMEM((length, width), jnp.bfloat16),
            pltpu.VMEM((length - 2 * HALO, hidden), jnp.bfloat16),
            pltpu.SemaphoreType.DMA((6,)),
        ],
        compiler_params=pltpu.CompilerParams(vmem_limit_bytes=26 * 1024 * 1024),
        name=f"tick{t}",
    )(flags, gain, gain_mlp, *operands)


def gather_rows(own):
    rows = lax.axis_size("y")
    far = rows // 2

    def swapped(value, mask):
        return lax.ppermute(value, "z", [(z, z ^ mask) for z in range(ZL)])

    def moved(value, delta):
        return lax.ppermute(value, "y", [(y, (y + delta) % rows) for y in range(rows)])

    def ring(chunks, steps):
        for step in steps:
            chunks[-step] = moved(chunks[1 - step], 1)
            chunks[step] = moved(chunks[step - 1], -1)

    near = {0: own}
    second, third = swapped(own, 2), swapped(own, 3)
    ring(near, range(1, far))
    near[far] = moved(near[1 - far], 1)
    second, third, _ = lax.optimization_barrier(
        (second, third, (near[far], near[1 - far], near[far - 1])))
    others = {0: jnp.stack([second, third])}
    ring(others, range(1, far))
    others[far] = moved(others[far - 1], -1)
    deltas = tuple(near)
    partner = swapped(jnp.stack([near[delta] for delta in deltas]), 1)
    stages = []
    for mine, theirs in ((deltas, (0, -1, 1)), ((), (-2, 2)), ((), (-3, 3, far))):
        pieces = [near[d] for d in mine] + [others[d] for d in theirs]
        spots = [((d, 0),) for d in mine] + [((d, 2), (d, 3)) for d in theirs]
        if len(stages) == 2:
            pieces.append(partner)
            spots.append(tuple((d, 1) for d in deltas))
        stages.append((pieces, spots))
    return stages, near, others


def body(
    fresh_tokens,
    fresh_mask,
    curve_order,
    held_state,
    held_mask,
    norm_gains,
    projections,
    mlp_gains,
    mlp_up,
    mlp_down,
):
    sections, seqs = lax.axis_size("section"), lax.axis_size(SEQ)
    is_first = lax.axis_index("section") == 0
    count, width = held_state.shape[1:]
    depth = projections.shape[2]

    own = jnp.stack([
        projections[0].transpose(1, 0, 2).reshape(depth, 4 * INNER),
        mlp_up[0],
        mlp_down[0],
    ])
    stages, near, others = gather_rows(own)
    flags = jnp.stack([
        is_first.astype(jnp.int32),
        lax.axis_index("y").astype(jnp.int32),
        lax.axis_index("z").astype(jnp.int32),
    ])
    shape = (3, seqs // ZL, ZL, depth, own.shape[2])

    up = [(i, i + 1) for i in range(seqs - 1)]
    down = [(i + 1, i) for i in range(seqs - 1)]

    def marked(mask):
        lines = jnp.pad(mask.astype(jnp.bfloat16), ((0, 0), (0, width - count)))[:, None]
        return jnp.broadcast_to(lines, (mask.shape[0], MARKS, width))

    _, held_state, held_mask = lax.optimization_barrier((others[-1], held_state, held_mask))
    main = jnp.concatenate([held_state, marked(held_mask)], axis=1)[0]
    payload = (lax.ppermute(main, SEQ, up), main, lax.ppermute(main, SEQ, down))

    local_order = curve_order - lax.axis_index(SEQ) * count
    serial_tokens = jax.vmap(lambda source, indices: jnp.take(source, indices, axis=0))(
        fresh_tokens, local_order
    )
    serial_mask = jnp.take_along_axis(fresh_mask, local_order, axis=1)
    every = ("section",) + SEQ
    lines = jnp.pad(
        serial_mask.astype(jnp.bfloat16), ((0, MARKS - TICKS + 1), (0, width - count)))
    lasts = jnp.concatenate([serial_tokens[0, count - HALO:], serial_tokens[1],
                             serial_tokens[2, count - HALO:], lines])
    firsts = jnp.concatenate([serial_tokens[0, :HALO], serial_tokens[1],
                              serial_tokens[2, :HALO], lines])
    lasts, firsts, _ = lax.optimization_barrier((lasts, firsts, others[-1]))
    feeds = (
        lax.ppermute(lasts, every, up),
        jnp.concatenate([serial_tokens, marked(serial_mask)], axis=1),
        lax.ppermute(firsts, every, down),
    )

    def relay(value, shift):
        return lax.ppermute(value, every, [
            (s * seqs + j, (s + 1) * seqs + j + shift)
            for s in range(sections - 1) for j in range(seqs) if 0 <= j + shift < seqs
        ])

    results = []
    weights = None
    for i, (pieces, spots) in enumerate(stages):
        weights = place(flags, weights, pieces, spots, shape, f"place{i}")
    for t in range(TICKS):
        outs = tick(t, flags, norm_gains, mlp_gains, payload, feeds, weights)
        results.append(outs[0])
        if t < TICKS - 1:
            shifts = (0,) if t % 2 == 0 else (1, 0, -1)
            payload = tuple(relay(outs[1], shift) for shift in shifts)
    return jnp.stack(results)[:, None]


def solution(mesh):
    sections, seqs = mesh.shape["section"], mesh.shape["seq"]
    split = Mesh(mesh.devices.reshape(sections, seqs // ZL, ZL), ("section",) + SEQ)
    return jax.shard_map(
        body,
        mesh=split,
        in_specs=(
            P(None, SEQ, None),
            P(None, SEQ),
            P(None, SEQ),
            P("section", SEQ, None),
            P("section", SEQ),
            P("section", None),
            P("section", None, SEQ, None),
            P("section", None),
            P("section", SEQ, None),
            P("section", SEQ, None),
        ),
        out_specs=P(None, "section", SEQ, None),
        check_vma=False,
    )
```

```python
import functools

import jax
import jax.numpy as jnp
from jax import lax
from jax.experimental import pallas as pl
from jax.experimental.pallas import tpu as pltpu
from jax.sharding import Mesh, PartitionSpec as P

HEADS = 8
HEAD = 64
INNER = 512
HALO = 64
TICKS = 4
ZL = 4
TILE = 512
MARKS = 16
SEQ = ("y", "z")


def _normed(values, gain):
    average = jnp.mean(values, axis=-1, keepdims=True)
    centered = values - average
    spread_sq = jnp.mean(centered * centered, axis=-1, keepdims=True)
    return (centered * lax.rsqrt(spread_sq + 1e-05) * gain).astype(jnp.bfloat16)


def _dot(a, b, dims):
    return lax.dot_general(a, b, (dims, ((), ())), preferred_element_type=jnp.float32)


def chunk_copies(flags_ref, weights, pieces, spots, sems):
    my_y, my_z = flags_ref[1], flags_ref[2]
    rows = weights.shape[1]
    flipped = my_z + 1 - 2 * lax.rem(my_z, 2)
    columns_at = (my_z, flipped, lax.rem(my_z + 2, ZL), ZL - 1 - my_z)
    found, slot = [], 0
    for piece, places in zip(pieces, spots):
        for i, (delta, mask) in enumerate(places):
            y = lax.rem(my_y + (delta + rows), rows)
            chunk = piece if len(piece.shape) == 3 else piece.at[i]
            found.append(pltpu.make_async_copy(
                chunk, weights.at[:, y, columns_at[mask]], sems.at[slot]))
            slot += 1
    return found


def place_kernel(spots, fresh, flags_ref, *refs):
    weights, sems = refs[-2:]
    pieces = refs[:-2] if fresh else refs[1:-2]
    copies = chunk_copies(flags_ref, weights, pieces, spots, sems)
    for copy in copies:
        copy.start()
    for copy in copies:
        copy.wait()


def place(flags, weights, pieces, spots, shape, name):
    fresh = weights is None
    anyw = pl.BlockSpec(memory_space=pl.ANY)
    held = [] if fresh else [weights]
    chunks = sum(len(p) for p in spots)
    moved_bytes = 2 * chunks * shape[0] * shape[3] * shape[4] * 2
    return pl.pallas_call(
        functools.partial(place_kernel, spots, fresh),
        out_shape=jax.ShapeDtypeStruct(shape, jnp.bfloat16),
        in_specs=[pl.BlockSpec(memory_space=pltpu.SMEM)] + [anyw] * (len(held) + len(pieces)),
        out_specs=anyw,
        input_output_aliases={} if fresh else {1: 0},
        scratch_shapes=[pltpu.SemaphoreType.DMA((chunks,))],
        compiler_params=pltpu.CompilerParams(vmem_limit_bytes=2 * 1024 * 1024),
        cost_estimate=pl.CostEstimate(flops=0, bytes_accessed=moved_bytes, transcendentals=0),
        name=name,
    )(flags, *held, *pieces)


def tick_kernel(t, flags_ref, gain_ref, gain_mlp_ref, *refs):
    broad = t % 2 == 0
    size = 3 if broad else 1
    relayed, refs = refs[:size], refs[size:]
    feeds = ()
    if t > 0:
        feeds, refs = refs[:3], refs[3:]
    weights, out_ref, refs = refs[0], refs[1], refs[2:]
    if t < TICKS - 1:
        onward_ref, refs = refs[0], refs[1:]
    qkv, context, marks, seen, normed, hidden, sems = refs
    count = out_ref.shape[0]
    edge = 2 * HALO if broad else HALO
    length = count + 2 * edge
    kept = length - 2 * HALO

    def shifted(lines, width):
        return pltpu.roll(lines, lines.shape[1] - HALO, 1)[:, :width]

    def joined():
        return jnp.concatenate(
            [marks[i, :, :count].astype(jnp.float32) for i in range(3)], axis=1)

    def arrived():
        if broad:
            for i, ref in enumerate(relayed):
                context[i * count:(i + 1) * count] = ref[:count]
                marks[i] = ref[count:]
            seen[...] = joined()
        else:
            context[:length] = relayed[0][:length]
            seen[:, :length] = relayed[0][length:, :length].astype(jnp.float32)

    if feeds:
        @pl.when(flags_ref[0] == 1)
        def _():
            before_ref, main_ref, after_ref = feeds
            at = (0, HALO, HALO + count)[t - 1]
            tail = before_ref.shape[0] - MARKS
            moves = (
                (before_ref.at[at:at + edge], context.at[:edge]),
                (main_ref.at[t - 1, :count], context.at[edge:edge + count]),
                (after_ref.at[at:at + edge], context.at[edge + count:length]),
                (before_ref.at[tail:], marks.at[0]),
                (main_ref.at[t - 1, count:], marks.at[1]),
                (after_ref.at[tail:], marks.at[2]),
            )
            fetched = [
                pltpu.make_async_copy(source, target, sems.at[i])
                for i, (source, target) in enumerate(moves)
            ]
            for copy in fetched:
                copy.start()
            for copy in fetched:
                copy.wait()
            if broad:
                seen[...] = joined()
            else:
                seen[:, :length] = shifted(joined(), length)

        pl.when(flags_ref[0] != 1)(arrived)
    else:
        arrived()

    pick = max(t - 1, 0)
    line = seen[pick:pick + 1, :length]
    for lo in range(0, length, count):
        normed[lo:lo + count] = _normed(context[lo:lo + count].astype(jnp.float32), gain_ref[...])

    def columns(a, lo, hi):
        return weights[a, :, :, :, lo:hi].reshape(-1, hi - lo)

    for n in range(3):
        qkv[:length, n * INNER:(n + 1) * INNER] = _dot(
            normed[:length], columns(0, n * INNER, (n + 1) * INNER), ((1,), (0,))
        ).astype(jnp.bfloat16)

    reach = count + 2 * HALO
    row = lax.broadcasted_iota(jnp.int32, (count, reach), 0)
    col = lax.broadcasted_iota(jnp.int32, (count, reach), 1) - HALO
    lane = lax.broadcasted_iota(jnp.int32, (count, 2 * HEAD), 1)
    for lo in range(0, kept, count):
        allowed = (jnp.abs(col - row) <= HALO) & ((line[:, lo:lo + reach] > 0.5) | (col == row))
        barred = jnp.where(allowed, 0.0, 1.0)
        barred = jnp.concatenate([barred, barred], axis=0) > 0.5
        for pair in range(HEADS // 2):
            at = pair * 2 * HEAD
            q = qkv[lo + HALO:lo + HALO + count, at:at + 2 * HEAD]
            k = qkv[lo:lo + reach, INNER + at:INNER + at + 2 * HEAD]
            v = qkv[lo:lo + reach, 2 * INNER + at:2 * INNER + at + 2 * HEAD]
            zero = jnp.zeros_like(q)
            both = jnp.concatenate(
                [jnp.where(lane < HEAD, q, zero), jnp.where(lane < HEAD, zero, q)], axis=0)
            scores = _dot(both, k, ((1,), (1,))) * HEAD ** (-0.5)
            scores = jnp.where(barred, jnp.float32(-1e30), scores)
            highest = jnp.max(scores, axis=-1, keepdims=True)
            exps = jnp.exp(scores - highest)
            totals = jnp.sum(exps, axis=-1, keepdims=True)
            shares = (exps / totals).astype(jnp.bfloat16)
            mixed = _dot(shares, v, ((1,), (0,)))
            hidden[lo:lo + count, at:at + 2 * HEAD] = jnp.where(
                lane < HEAD, mixed[:count], mixed[count:]).astype(jnp.bfloat16)
    attended = context[HALO:HALO + kept].astype(jnp.float32) + _dot(
        hidden[:kept, :INNER], columns(0, 3 * INNER, 4 * INNER), ((1,), (1,)))
    attended = attended.astype(jnp.bfloat16)
    context[:kept] = attended
    normed[:kept] = _normed(attended.astype(jnp.float32), gain_mlp_ref[...])
    for lo in range(0, hidden.shape[1], TILE):
        up = _dot(normed[:kept], columns(1, lo, lo + TILE), ((1,), (0,)))
        up = 0.5 * up * (1.0 + lax.erf(up * (0.5 ** 0.5)))
        hidden[:kept, lo:lo + TILE] = up.astype(jnp.bfloat16)
    first = edge - HALO
    for g in range(0, weights.shape[1], 2):
        w = weights[2, g:g + 2]
        w = w.reshape(-1, w.shape[-1])
        size = w.shape[0]
        lo = g * size // 2
        result = (context[:kept, lo:lo + size].astype(jnp.float32) + _dot(
            hidden[:kept], w, ((1,), (1,)))).astype(jnp.bfloat16)
        out_ref[:, lo:lo + size] = result[first:first + count]
        if t < TICKS - 1:
            onward_ref[:kept, lo:lo + size] = result
    if t < TICKS - 1:
        onward_ref[kept:] = jnp.zeros((MARKS, onward_ref.shape[1]), onward_ref.dtype)
        lines = jnp.broadcast_to(line, (MARKS, length))
        onward_ref[kept:, :kept] = shifted(lines, kept).astype(onward_ref.dtype)


def tick(t, flags, gain, gain_mlp, payload, feeds, weights):
    width, hidden = payload[0].shape[1], weights.shape[-1]
    broad = t % 2 == 0
    count = payload[0].shape[0] - MARKS - (0 if broad else 2 * HALO)
    length = count + (4 if broad else 2) * HALO
    vmem = pl.BlockSpec(memory_space=pltpu.VMEM)
    anyw = pl.BlockSpec(memory_space=pl.ANY)
    outs = [jax.ShapeDtypeStruct((count, width), jnp.bfloat16)]
    if t < TICKS - 1:
        outs.append(jax.ShapeDtypeStruct((length - 2 * HALO + MARKS, width), jnp.bfloat16))
    operands = list(payload) + list(feeds if t > 0 else ()) + [weights]
    specs = [vmem] * len(payload) + [anyw] * (len(operands) - len(payload) - 1) + [vmem]
    return pl.pallas_call(
        functools.partial(tick_kernel, t),
        out_shape=tuple(outs),
        in_specs=[pl.BlockSpec(memory_space=pltpu.SMEM), vmem, vmem] + specs,
        out_specs=tuple([vmem] * len(outs)),
        scratch_shapes=[
            pltpu.VMEM((length, 3 * INNER), jnp.bfloat16),
            pltpu.VMEM((length, width), jnp.bfloat16),
            pltpu.VMEM((3, MARKS, width), jnp.bfloat16),
            pltpu.VMEM((MARKS, length if broad else count + 4 * HALO), jnp.float32),
            pltpu.VMEM((length, width), jnp.bfloat16),
            pltpu.VMEM((length - 2 * HALO, hidden), jnp.bfloat16),
            pltpu.SemaphoreType.DMA((6,)),
        ],
        compiler_params=pltpu.CompilerParams(vmem_limit_bytes=22 * 1024 * 1024),
        name=f"tick{t}",
    )(flags, gain, gain_mlp, *operands)


def gather_rows(own, early):
    rows = lax.axis_size("y")
    far = rows // 2

    def swapped(value, mask):
        return lax.ppermute(value, "z", [(z, z ^ mask) for z in range(ZL)])

    def moved(value, delta):
        return lax.ppermute(value, "y", [(y, (y + delta) % rows) for y in range(rows)])

    def ring(chunks, steps):
        for step in steps:
            chunks[-step] = moved(chunks[1 - step], 1)
            chunks[step] = moved(chunks[step - 1], -1)

    near = {0: own}
    second, third = swapped(own, 2), swapped(own, 3)
    ring(near, range(1, far))
    near[far] = moved(near[1 - far], 1)
    second, third, _, early = lax.optimization_barrier(
        (second, third, (near[1 - far], near[far - 1]), early))
    others = {0: jnp.stack([second, third])}
    ring(others, range(1, far))
    others[far] = moved(others[far - 1], -1)
    deltas = tuple(near)
    partner = swapped(jnp.stack([near[delta] for delta in deltas]), 1)
    stages = []
    for mine, theirs in ((deltas, (0, -1, 1)), ((), (-2, 2)), ((), (-3, 3, far))):
        pieces = [near[d] for d in mine] + [others[d] for d in theirs]
        spots = [((d, 0),) for d in mine] + [((d, 2), (d, 3)) for d in theirs]
        if len(stages) == 2:
            pieces.append(partner)
            spots.append(tuple((d, 1) for d in deltas))
        stages.append((pieces, spots))
    return stages, others, early


def body(
    fresh_tokens,
    fresh_mask,
    curve_order,
    held_state,
    held_mask,
    norm_gains,
    projections,
    mlp_gains,
    mlp_up,
    mlp_down,
):
    sections, seqs = lax.axis_size("section"), lax.axis_size(SEQ)
    is_first = lax.axis_index("section") == 0
    count, width = held_state.shape[1:]
    depth = projections.shape[2]

    own = jnp.stack([
        projections[0].transpose(1, 0, 2).reshape(depth, 4 * INNER),
        mlp_up[0],
        mlp_down[0],
    ])
    local_order = curve_order - lax.axis_index(SEQ) * count
    serial_tokens = jax.vmap(lambda source, indices: jnp.take(source, indices, axis=0))(
        fresh_tokens, local_order
    )
    serial_mask = jnp.take_along_axis(fresh_mask, local_order, axis=1)
    stages, others, (serial_tokens, serial_mask) = gather_rows(own, (serial_tokens, serial_mask))
    flags = jnp.stack([
        is_first.astype(jnp.int32),
        lax.axis_index("y").astype(jnp.int32),
        lax.axis_index("z").astype(jnp.int32),
    ])
    shape = (3, seqs // ZL, ZL, depth, own.shape[2])

    up = [(i, i + 1) for i in range(seqs - 1)]
    down = [(i + 1, i) for i in range(seqs - 1)]

    def marked(mask):
        lines = jnp.pad(mask.astype(jnp.bfloat16), ((0, 0), (0, width - count)))[:, None]
        return jnp.broadcast_to(lines, (mask.shape[0], MARKS, width))

    _, held_state, held_mask = lax.optimization_barrier((others[-1], held_state, held_mask))
    main = jnp.concatenate([held_state, marked(held_mask)], axis=1)[0]
    payload = (lax.ppermute(main, SEQ, up), main, lax.ppermute(main, SEQ, down))

    every = ("section",) + SEQ
    lines = jnp.pad(
        serial_mask.astype(jnp.bfloat16), ((0, MARKS - TICKS + 1), (0, width - count)))
    lasts = jnp.concatenate([serial_tokens[0, count - HALO:], serial_tokens[1],
                             serial_tokens[2, count - HALO:], lines])
    firsts = jnp.concatenate([serial_tokens[0, :HALO], serial_tokens[1],
                              serial_tokens[2, :HALO], lines])
    lasts, firsts, _ = lax.optimization_barrier((lasts, firsts, others[-1]))
    feeds = (
        lax.ppermute(lasts, every, up),
        jnp.concatenate([serial_tokens, marked(serial_mask)], axis=1),
        lax.ppermute(firsts, every, down),
    )

    results = []
    weights = None
    for i, (pieces, spots) in enumerate(stages):
        weights = place(flags, weights, pieces, spots, shape, f"place{i}")
    for t in range(TICKS):
        outs = tick(t, flags, norm_gains, mlp_gains, payload, feeds, weights)
        results.append(outs[0])
        if t < TICKS - 1:
            main = lax.ppermute(
                outs[1], "section", [(i, i + 1) for i in range(sections - 1)])
            payload = (main,) if t % 2 == 0 else (
                lax.ppermute(main, SEQ, up), main, lax.ppermute(main, SEQ, down))
    return jnp.stack(results)[:, None]


def solution(mesh):
    sections, seqs = mesh.shape["section"], mesh.shape["seq"]
    split = Mesh(mesh.devices.reshape(sections, seqs // ZL, ZL), ("section",) + SEQ)
    return jax.shard_map(
        body,
        mesh=split,
        in_specs=(
            P(None, SEQ, None),
            P(None, SEQ),
            P(None, SEQ),
            P("section", SEQ, None),
            P("section", SEQ),
            P("section", None),
            P("section", None, SEQ, None),
            P("section", None),
            P("section", SEQ, None),
            P("section", SEQ, None),
        ),
        out_specs=P(None, "section", SEQ, None),
        check_vma=False,
    )
```

```python
import functools

import jax
import jax.numpy as jnp
from jax import lax
from jax.experimental import pallas as pl
from jax.experimental.pallas import tpu as pltpu
from jax.sharding import Mesh, PartitionSpec as P

HEADS = 8
HEAD = 64
INNER = 512
HALO = 64
TICKS = 4
ZL = 4
TILE = 512
MARKS = 16
SEQ = ("y", "z")


def _normed(values, gain):
    average = jnp.mean(values, axis=-1, keepdims=True)
    centered = values - average
    spread_sq = jnp.mean(centered * centered, axis=-1, keepdims=True)
    return (centered * lax.rsqrt(spread_sq + 1e-05) * gain).astype(jnp.bfloat16)


def _dot(a, b, dims):
    return lax.dot_general(a, b, (dims, ((), ())), preferred_element_type=jnp.float32)


def chunk_copies(flags_ref, weights, pieces, spots, sems):
    my_y, my_z = flags_ref[1], flags_ref[2]
    rows = weights.shape[1]
    flipped = my_z + 1 - 2 * lax.rem(my_z, 2)
    columns_at = (my_z, flipped, lax.rem(my_z + 2, ZL), ZL - 1 - my_z)
    found, slot = [], 0
    for piece, places in zip(pieces, spots):
        for i, (delta, mask) in enumerate(places):
            y = lax.rem(my_y + (delta + rows), rows)
            chunk = piece if len(piece.shape) == 3 else piece.at[i]
            found.append(pltpu.make_async_copy(
                chunk, weights.at[:, y, columns_at[mask]], sems.at[slot]))
            slot += 1
    return found


def place_kernel(spots, fresh, flags_ref, *refs):
    weights, sems = refs[-2:]
    pieces = refs[:-2] if fresh else refs[1:-2]
    copies = chunk_copies(flags_ref, weights, pieces, spots, sems)
    for copy in copies:
        copy.start()
    for copy in copies:
        copy.wait()


def place(flags, weights, pieces, spots, shape, name):
    fresh = weights is None
    anyw = pl.BlockSpec(memory_space=pl.ANY)
    held = [] if fresh else [weights]
    chunks = sum(len(p) for p in spots)
    moved_bytes = 2 * chunks * shape[0] * shape[3] * shape[4] * 2
    return pl.pallas_call(
        functools.partial(place_kernel, spots, fresh),
        out_shape=jax.ShapeDtypeStruct(shape, jnp.bfloat16),
        in_specs=[pl.BlockSpec(memory_space=pltpu.SMEM)] + [anyw] * (len(held) + len(pieces)),
        out_specs=anyw,
        input_output_aliases={} if fresh else {1: 0},
        scratch_shapes=[pltpu.SemaphoreType.DMA((chunks,))],
        compiler_params=pltpu.CompilerParams(vmem_limit_bytes=2 * 1024 * 1024),
        cost_estimate=pl.CostEstimate(flops=0, bytes_accessed=moved_bytes, transcendentals=0),
        name=name,
    )(flags, *held, *pieces)


def tick_kernel(t, flags_ref, gain_ref, gain_mlp_ref, *refs):
    broad = t % 2 == 0
    size = 3 if broad else 1
    relayed, refs = refs[:size], refs[size:]
    feeds = ()
    if t > 0:
        feeds, refs = refs[:3], refs[3:]
    weights, out_ref, refs = refs[0], refs[1], refs[2:]
    if t < TICKS - 1:
        onward_ref, refs = refs[0], refs[1:]
    qkv, context, marks, seen, normed, hidden, sems = refs
    count = out_ref.shape[0]
    edge = 2 * HALO if broad else HALO
    length = count + 2 * edge
    kept = length - 2 * HALO

    def shifted(lines, width):
        return pltpu.roll(lines, lines.shape[1] - HALO, 1)[:, :width]

    def joined():
        return jnp.concatenate(
            [marks[i, :, :count].astype(jnp.float32) for i in range(3)], axis=1)

    def arrived():
        if broad:
            for i, ref in enumerate(relayed):
                context[i * count:(i + 1) * count] = ref[:count]
                marks[i] = ref[count:]
            seen[...] = joined()
        else:
            context[:length] = relayed[0][:length]
            seen[:, :length] = relayed[0][length:, :length].astype(jnp.float32)

    if feeds:
        @pl.when(flags_ref[0] == 1)
        def _():
            before_ref, main_ref, after_ref = feeds
            at = (0, HALO, HALO + count)[t - 1]
            tail = before_ref.shape[0] - MARKS
            moves = (
                (before_ref.at[at:at + edge], context.at[:edge]),
                (main_ref.at[t - 1, :count], context.at[edge:edge + count]),
                (after_ref.at[at:at + edge], context.at[edge + count:length]),
                (before_ref.at[tail:], marks.at[0]),
                (main_ref.at[t - 1, count:], marks.at[1]),
                (after_ref.at[tail:], marks.at[2]),
            )
            fetched = [
                pltpu.make_async_copy(source, target, sems.at[i])
                for i, (source, target) in enumerate(moves)
            ]
            for copy in fetched:
                copy.start()
            for copy in fetched:
                copy.wait()
            if broad:
                seen[...] = joined()
            else:
                seen[:, :length] = shifted(joined(), length)

        pl.when(flags_ref[0] != 1)(arrived)
    else:
        arrived()

    pick = max(t - 1, 0)
    line = seen[pick:pick + 1, :length]
    for lo in range(0, length, count):
        normed[lo:lo + count] = _normed(context[lo:lo + count].astype(jnp.float32), gain_ref[...])

    def columns(a, lo, hi):
        return weights[a, :, :, :, lo:hi].reshape(-1, hi - lo)

    for n in range(3):
        qkv[:length, n * INNER:(n + 1) * INNER] = _dot(
            normed[:length], columns(0, n * INNER, (n + 1) * INNER), ((1,), (0,))
        ).astype(jnp.bfloat16)

    reach = count + 2 * HALO
    row = lax.broadcasted_iota(jnp.int32, (count, reach), 0)
    col = lax.broadcasted_iota(jnp.int32, (count, reach), 1) - HALO
    lane = lax.broadcasted_iota(jnp.int32, (count, 2 * HEAD), 1)
    for lo in range(0, kept, count):
        allowed = (jnp.abs(col - row) <= HALO) & ((line[:, lo:lo + reach] > 0.5) | (col == row))
        barred = jnp.where(allowed, 0.0, 1.0)
        barred = jnp.concatenate([barred, barred], axis=0) > 0.5
        for pair in range(HEADS // 2):
            at = pair * 2 * HEAD
            q = qkv[lo + HALO:lo + HALO + count, at:at + 2 * HEAD]
            k = qkv[lo:lo + reach, INNER + at:INNER + at + 2 * HEAD]
            v = qkv[lo:lo + reach, 2 * INNER + at:2 * INNER + at + 2 * HEAD]
            zero = jnp.zeros_like(q)
            both = jnp.concatenate(
                [jnp.where(lane < HEAD, q, zero), jnp.where(lane < HEAD, zero, q)], axis=0)
            scores = _dot(both, k, ((1,), (1,))) * HEAD ** (-0.5)
            scores = jnp.where(barred, jnp.float32(-1e30), scores)
            highest = jnp.max(scores, axis=-1, keepdims=True)
            exps = jnp.exp(scores - highest)
            totals = jnp.sum(exps, axis=-1, keepdims=True)
            shares = (exps / totals).astype(jnp.bfloat16)
            mixed = _dot(shares, v, ((1,), (0,)))
            hidden[lo:lo + count, at:at + 2 * HEAD] = jnp.where(
                lane < HEAD, mixed[:count], mixed[count:]).astype(jnp.bfloat16)
    attended = context[HALO:HALO + kept].astype(jnp.float32) + _dot(
        hidden[:kept, :INNER], columns(0, 3 * INNER, 4 * INNER), ((1,), (1,)))
    attended = attended.astype(jnp.bfloat16)
    context[:kept] = attended
    normed[:kept] = _normed(attended.astype(jnp.float32), gain_mlp_ref[...])
    for lo in range(0, hidden.shape[1], TILE):
        up = _dot(normed[:kept], columns(1, lo, lo + TILE), ((1,), (0,)))
        up = 0.5 * up * (1.0 + lax.erf(up * (0.5 ** 0.5)))
        hidden[:kept, lo:lo + TILE] = up.astype(jnp.bfloat16)
    first = edge - HALO
    for g in range(0, weights.shape[1], 2):
        w = weights[2, g:g + 2]
        w = w.reshape(-1, w.shape[-1])
        size = w.shape[0]
        lo = g * size // 2
        result = (context[:kept, lo:lo + size].astype(jnp.float32) + _dot(
            hidden[:kept], w, ((1,), (1,)))).astype(jnp.bfloat16)
        out_ref[:, lo:lo + size] = result[first:first + count]
        if t < TICKS - 1:
            onward_ref[:kept, lo:lo + size] = result
    if t < TICKS - 1:
        onward_ref[kept:] = jnp.zeros((MARKS, onward_ref.shape[1]), onward_ref.dtype)
        lines = jnp.broadcast_to(line, (MARKS, length))
        onward_ref[kept:, :kept] = shifted(lines, kept).astype(onward_ref.dtype)


def tick(t, flags, gain, gain_mlp, payload, feeds, weights):
    width, hidden = payload[0].shape[1], weights.shape[-1]
    broad = t % 2 == 0
    count = payload[0].shape[0] - MARKS - (0 if broad else 2 * HALO)
    length = count + (4 if broad else 2) * HALO
    vmem = pl.BlockSpec(memory_space=pltpu.VMEM)
    anyw = pl.BlockSpec(memory_space=pl.ANY)
    outs = [jax.ShapeDtypeStruct((count, width), jnp.bfloat16)]
    if t < TICKS - 1:
        outs.append(jax.ShapeDtypeStruct((length - 2 * HALO + MARKS, width), jnp.bfloat16))
    operands = list(payload) + list(feeds if t > 0 else ()) + [weights]
    specs = [vmem] * len(payload) + [anyw] * (len(operands) - len(payload) - 1) + [vmem]
    return pl.pallas_call(
        functools.partial(tick_kernel, t),
        out_shape=tuple(outs),
        in_specs=[pl.BlockSpec(memory_space=pltpu.SMEM), vmem, vmem] + specs,
        out_specs=tuple([vmem] * len(outs)),
        scratch_shapes=[
            pltpu.VMEM((length, 3 * INNER), jnp.bfloat16),
            pltpu.VMEM((length, width), jnp.bfloat16),
            pltpu.VMEM((3, MARKS, width), jnp.bfloat16),
            pltpu.VMEM((MARKS, length if broad else count + 4 * HALO), jnp.float32),
            pltpu.VMEM((length, width), jnp.bfloat16),
            pltpu.VMEM((length - 2 * HALO, hidden), jnp.bfloat16),
            pltpu.SemaphoreType.DMA((6,)),
        ],
        compiler_params=pltpu.CompilerParams(vmem_limit_bytes=22 * 1024 * 1024),
        name=f"tick{t}",
    )(flags, gain, gain_mlp, *operands)


def gather_rows(own):
    rows = lax.axis_size("y")
    far = rows // 2

    def swapped(value, mask):
        return lax.ppermute(value, "z", [(z, z ^ mask) for z in range(ZL)])

    def moved(value, delta):
        return lax.ppermute(value, "y", [(y, (y + delta) % rows) for y in range(rows)])

    def ring(chunks, steps):
        for step in steps:
            chunks[-step] = moved(chunks[1 - step], 1)
            chunks[step] = moved(chunks[step - 1], -1)

    near = {0: own}
    second, third = swapped(own, 2), swapped(own, 3)
    ring(near, range(1, far))
    near[far] = moved(near[1 - far], 1)
    second, third, _ = lax.optimization_barrier(
        (second, third, (near[far], near[1 - far], near[far - 1])))
    others = {0: jnp.stack([second, third])}
    ring(others, range(1, far))
    others[far] = moved(others[far - 1], -1)
    deltas = tuple(near)
    partner = swapped(jnp.stack([near[delta] for delta in deltas]), 1)
    stages = []
    for mine, theirs in ((deltas, (0, -1, 1)), ((), (-2, 2)), ((), (-3, 3, far))):
        pieces = [near[d] for d in mine] + [others[d] for d in theirs]
        spots = [((d, 0),) for d in mine] + [((d, 2), (d, 3)) for d in theirs]
        if len(stages) == 2:
            pieces.append(partner)
            spots.append(tuple((d, 1) for d in deltas))
        stages.append((pieces, spots))
    return stages, near, others


def body(
    fresh_tokens,
    fresh_mask,
    curve_order,
    held_state,
    held_mask,
    norm_gains,
    projections,
    mlp_gains,
    mlp_up,
    mlp_down,
):
    sections, seqs = lax.axis_size("section"), lax.axis_size(SEQ)
    is_first = lax.axis_index("section") == 0
    count, width = held_state.shape[1:]
    depth = projections.shape[2]

    own = jnp.stack([
        projections[0].transpose(1, 0, 2).reshape(depth, 4 * INNER),
        mlp_up[0],
        mlp_down[0],
    ])
    stages, near, others = gather_rows(own)
    flags = jnp.stack([
        is_first.astype(jnp.int32),
        lax.axis_index("y").astype(jnp.int32),
        lax.axis_index("z").astype(jnp.int32),
    ])
    shape = (3, seqs // ZL, ZL, depth, own.shape[2])

    up = [(i, i + 1) for i in range(seqs - 1)]
    down = [(i + 1, i) for i in range(seqs - 1)]

    def marked(mask):
        lines = jnp.pad(mask.astype(jnp.bfloat16), ((0, 0), (0, width - count)))[:, None]
        return jnp.broadcast_to(lines, (mask.shape[0], MARKS, width))

    _, held_state, held_mask = lax.optimization_barrier((others[-1], held_state, held_mask))
    main = jnp.concatenate([held_state, marked(held_mask)], axis=1)[0]
    payload = (lax.ppermute(main, SEQ, up), main, lax.ppermute(main, SEQ, down))

    local_order = curve_order - lax.axis_index(SEQ) * count
    serial_tokens = jax.vmap(lambda source, indices: jnp.take(source, indices, axis=0))(
        fresh_tokens, local_order
    )
    serial_mask = jnp.take_along_axis(fresh_mask, local_order, axis=1)
    every = ("section",) + SEQ
    lines = jnp.pad(
        serial_mask.astype(jnp.bfloat16), ((0, MARKS - TICKS + 1), (0, width - count)))
    lasts = jnp.concatenate([serial_tokens[0, count - HALO:], serial_tokens[1],
                             serial_tokens[2, count - HALO:], lines])
    firsts = jnp.concatenate([serial_tokens[0, :HALO], serial_tokens[1],
                              serial_tokens[2, :HALO], lines])
    lasts, firsts, _ = lax.optimization_barrier((lasts, firsts, others[-1]))
    feeds = (
        lax.ppermute(lasts, every, up),
        jnp.concatenate([serial_tokens, marked(serial_mask)], axis=1),
        lax.ppermute(firsts, every, down),
    )

    def relay(value, shift):
        return lax.ppermute(value, every, [
            (s * seqs + j, (s + 1) * seqs + j + shift)
            for s in range(sections - 1) for j in range(seqs) if 0 <= j + shift < seqs
        ])

    results = []
    weights = None
    for i, (pieces, spots) in enumerate(stages):
        weights = place(flags, weights, pieces, spots, shape, f"place{i}")
    for t in range(TICKS):
        outs = tick(t, flags, norm_gains, mlp_gains, payload, feeds, weights)
        results.append(outs[0])
        if t < TICKS - 1:
            shifts = (0,) if t % 2 == 0 else (1, 0, -1)
            payload = tuple(relay(outs[1], shift) for shift in shifts)
    return jnp.stack(results)[:, None]


def solution(mesh):
    sections, seqs = mesh.shape["section"], mesh.shape["seq"]
    split = Mesh(mesh.devices.reshape(sections, seqs // ZL, ZL), ("section",) + SEQ)
    return jax.shard_map(
        body,
        mesh=split,
        in_specs=(
            P(None, SEQ, None),
            P(None, SEQ),
            P(None, SEQ),
            P("section", SEQ, None),
            P("section", SEQ),
            P("section", None),
            P("section", None, SEQ, None),
            P("section", None),
            P("section", SEQ, None),
            P("section", SEQ, None),
        ),
        out_specs=P(None, "section", SEQ, None),
        check_vma=False,
    )
```
